32 devices in a mesh: tensor: 2 (over y), context: 16 (over z, x, core).
Axes of the slice: x: 2, y: 2, z: 4, core: 2. Of those that a mesh axis runs over, the one named last changes fastest.
Arguments:
- hidden_in: bfloat16 [8192, 4096], P('context', 'tensor'), may hold values from -6 to 6
- norm_gain: bfloat16 [4096], replicated, may hold values from 0.099609375 to 1.8984375
- w_query: bfloat16 [4096, 4096], P('context', 'tensor'), may hold values from -0.09375 to 0.09375
- w_key: bfloat16 [4096, 1024], P('context', 'tensor'), may hold values from -0.09375 to 0.09375
- w_value: bfloat16 [4096, 1024], P('context', 'tensor'), may hold values from -0.09375 to 0.09375
- kv_cache: bfloat16 [16384, 2, 1024], P('context', None, 'tensor'), may hold values from -68 to 68
- selected: int32 [16, 3], replicated, may hold values from 0 to 127, as said below
Outputs:
- attended: bfloat16 [8192, 4096], P('context', 'tensor')
The draws below stay inside these ranges and needn't reach their ends.
Inputs may be any that keep to these rules, and one draw needn't show every extreme that they name: `selected`: each row names 3 cache blocks held by 3 different devices of context (block c is held by device c // 8). The blocks held by one device are named at most 6 times over all rows together, and those of one device exactly 6 times.
All inputs are finite; a program needn't handle non-finite values.
Results may differ from the reference program's by a relative error of at most 0.011.
The reference program's roundings to bfloat16 on the way (of `normed`, `query` and `probs`) count: a program that leaves them out, or rounds other values in their place, can miss the bound.
Values may be sent and summed in bfloat16 or wider, within the bound.
A program may use at most 128 MiB of HBM per device.

```python
import math
import jax
import jax.numpy as jnp
from jax import lax

D = 4096
HEADS = 32
KV_HEADS = 8
HEAD_DIM = 128
Q_BLOCK = 512
C_BLOCK = 128
PICKS = 3
MOST_REQ = 6
BLOCKS_DEV = 8
TOKENS = 8192
CACHE_BLOCKS = 128
CACHE_TOKENS = 16384
N_CONTEXT = 16


def draw_kv_cache(key, part):
    first_key = jax.random.fold_in(key, 0)
    array_shape = (CACHE_BLOCKS, C_BLOCK, 2, KV_HEADS, HEAD_DIM)
    values = jnp.clip(jax.random.normal(first_key, array_shape, jnp.float32), -4.0, 4.0)
    return values.reshape(CACHE_TOKENS, 2, KV_HEADS * HEAD_DIM).astype(jnp.bfloat16)


def draw_selected(key, part):
    devices = N_CONTEXT
    key_hot, key_order, key_offset, key_rows = jax.random.split(key, 4)
    hottest = jax.random.randint(key_hot, (), 0, devices)
    others = jax.random.permutation(key_order, devices - 1)
    others = others + (others >= hottest).astype(jnp.int32)
    serial = jnp.arange(devices * PICKS, dtype=jnp.int32).reshape(PICKS, devices)
    spot = jnp.mod(serial - MOST_REQ, devices - 1)
    holder = jnp.where(serial < MOST_REQ, hottest, others[spot])
    offset = jax.random.randint(key_offset, (PICKS, devices), 0, BLOCKS_DEV)
    shuffle = jax.random.permutation(key_rows, devices)
    numbers = (holder * BLOCKS_DEV + offset)[:, shuffle]
    return numbers.T.astype(jnp.int32)


def shard_levels(rng, shape, shards, low, top_value):
    level = 1.0
    for axis_at, parts in shards:
        draws = jax.random.uniform(jax.random.fold_in(jax.random.fold_in(rng, 6), axis_at), (parts,), jnp.float32, low / len(shards), top_value / len(shards))
        level = level * jnp.repeat(jnp.exp(draws), shape[axis_at] // parts).reshape((-1,) + (1,) * (len(shape) - 1 - axis_at))
    return level


def bell_draw(key, dims, scale, reach, pieces=(), held_as=jnp.bfloat16):
    factor_of = shard_levels(key, dims, pieces, -0.22, 0.18) if pieces else 1.0
    drawn = jax.random.normal(key, dims, jnp.float32) * scale * factor_of
    return jnp.minimum(jnp.maximum(drawn, -reach), reach).astype(held_as)


def setup_inputs(seed: int = 0) -> dict:
    key_list = jax.random.split(jax.random.key(seed), 8)
    hidden_in = bell_draw(key_list[0], (TOKENS, D), 1.0, 6.0, ((0, 16), (1, 2)))
    norm_gain = jnp.clip(1.0 + 0.18 * jax.random.normal(key_list[1], (D,), jnp.float32), 0.099609375, 1.8984375).astype(jnp.bfloat16)
    w_query = bell_draw(key_list[2], (D, HEADS * HEAD_DIM), D ** -0.5, 0.09375, ((0, 16), (1, 2)))
    w_key = bell_draw(key_list[3], (D, KV_HEADS * HEAD_DIM), D ** -0.5, 0.09375, ((0, 16), (1, 2)))
    w_value = bell_draw(key_list[4], (D, KV_HEADS * HEAD_DIM), D ** -0.5, 0.09375, ((0, 16), (1, 2)))
    kv_cache = draw_kv_cache(jax.random.fold_in(key_list[7], 71), 0)
    selected = draw_selected(jax.random.fold_in(key_list[7], 71), 0)
    return {"hidden_in": hidden_in, "norm_gain": norm_gain, "w_query": w_query, "w_key": w_key, "w_value": w_value, "kv_cache": kv_cache, "selected": selected}


def reference(hidden_in, norm_gain, w_query, w_key, w_value, kv_cache, selected):
    floats = hidden_in.astype(jnp.float32)
    inverse_rms = lax.rsqrt(lax.optimization_barrier(jnp.mean(floats * floats, axis=1, keepdims=True)) + 1e-05)
    normed = (floats * inverse_rms * norm_gain.astype(jnp.float32)).astype(jnp.bfloat16)
    query = jnp.dot(normed, w_query, preferred_element_type=jnp.float32).astype(jnp.bfloat16)
    fresh_key = jnp.dot(normed, w_key, preferred_element_type=jnp.float32).astype(jnp.bfloat16)
    fresh_value = jnp.dot(normed, w_value, preferred_element_type=jnp.float32).astype(jnp.bfloat16)
    groups = HEADS // KV_HEADS
    blocks = kv_cache.reshape(CACHE_BLOCKS, C_BLOCK, 2, KV_HEADS, HEAD_DIM)
    cached = PICKS * C_BLOCK
    score_scale = 1.0 / math.sqrt(HEAD_DIM)
    row_index = jnp.arange(Q_BLOCK, dtype=jnp.int32)[:, None]
    col_index = jnp.arange(cached + Q_BLOCK, dtype=jnp.int32)[None, :]
    visible = (col_index < cached) | (col_index - cached <= row_index)

    def one_block(block_number):
        start = block_number * Q_BLOCK
        query_rows = lax.dynamic_slice_in_dim(query, start, Q_BLOCK, 0).reshape(Q_BLOCK, KV_HEADS, groups, HEAD_DIM)
        key_rows = lax.dynamic_slice_in_dim(fresh_key, start, Q_BLOCK, 0).reshape(Q_BLOCK, KV_HEADS, HEAD_DIM)
        value_rows = lax.dynamic_slice_in_dim(fresh_value, start, Q_BLOCK, 0).reshape(Q_BLOCK, KV_HEADS, HEAD_DIM)
        chosen = jnp.take(blocks, selected[block_number], axis=0)
        keys_all = jnp.concatenate([chosen[:, :, 0].reshape(cached, KV_HEADS, HEAD_DIM), key_rows], axis=0)
        values_all = jnp.concatenate([chosen[:, :, 1].reshape(cached, KV_HEADS, HEAD_DIM), value_rows], axis=0)
        scores = jnp.einsum('qhgd,khd->hgqk', query_rows.astype(jnp.float32), keys_all.astype(jnp.float32)) * score_scale
        scores = jnp.where(visible[None, None], scores, -jnp.inf)
        probs = jax.nn.softmax(scores, axis=-1).astype(jnp.bfloat16)
        output = jnp.einsum('hgqk,khd->qhgd', probs.astype(jnp.float32), values_all.astype(jnp.float32))
        return output.astype(jnp.bfloat16).reshape(Q_BLOCK, HEADS * HEAD_DIM)
    results = lax.map(one_block, jnp.arange(N_CONTEXT, dtype=jnp.int32))
    return results.reshape(TOKENS, HEADS * HEAD_DIM)
```

```python
import functools
import math

import jax
import jax.numpy as jnp
from jax import lax
from jax.experimental import pallas as pl
from jax.experimental.pallas import tpu as pltpu
from jax.sharding import PartitionSpec as P

HEAD_DIM = 128
C_BLOCK = 128
PICKS = 3
MOST_REQ = 6
BLOCKS_DEV = 8
ROW_TILE = 256


def attend_kernel(groups, q_ref, k_ref, v_ref, ck_ref, cv_ref, o_ref):
    rows = q_ref.shape[0]
    tile = min(ROW_TILE, rows)
    factor = math.log2(math.e) / math.sqrt(HEAD_DIM)
    dims = (((1,), (1,)), ((), ()))
    for head in range(groups):
        place = slice(head * HEAD_DIM, (head + 1) * HEAD_DIM)
        for start in range(0, rows, tile):
            stop = start + tile
            query = q_ref[start:stop, place]
            cached = lax.dot_general(query, ck_ref[...], dims, preferred_element_type=jnp.float32)
            fresh = lax.dot_general(query, k_ref[:stop, :], dims, preferred_element_type=jnp.float32)
            row = lax.broadcasted_iota(jnp.int32, fresh.shape, 0) + start
            col = lax.broadcasted_iota(jnp.int32, fresh.shape, 1)
            fresh = jnp.where(col <= row, fresh, -jnp.inf)
            top = jnp.maximum(
                jnp.max(cached, axis=1, keepdims=True), jnp.max(fresh, axis=1, keepdims=True)
            )
            cached = jnp.exp2((cached - top) * factor)
            fresh = jnp.exp2((fresh - top) * factor)
            total = jnp.sum(cached, axis=1, keepdims=True) + jnp.sum(fresh, axis=1, keepdims=True)
            inverse = 1.0 / total
            mixed = jnp.dot(
                (cached * inverse).astype(jnp.bfloat16),
                cv_ref[...],
                preferred_element_type=jnp.float32,
            )
            mixed += jnp.dot(
                (fresh * inverse).astype(jnp.bfloat16),
                v_ref[:stop, :],
                preferred_element_type=jnp.float32,
            )
            o_ref[start:stop, place] = mixed.astype(o_ref.dtype)


def attend(projected, cached_key, cached_value, groups, local_heads):
    rows = projected.shape[0]
    cached = cached_key.shape[0]
    heads = groups * local_heads
    block = lambda height, width, place: pl.BlockSpec((height, width), lambda g: (0, place(g)))
    return pl.pallas_call(
        functools.partial(attend_kernel, groups),
        grid=(local_heads,),
        out_shape=jax.ShapeDtypeStruct((rows, heads * HEAD_DIM), jnp.bfloat16),
        in_specs=[
            block(rows, groups * HEAD_DIM, lambda g: g),
            block(rows, HEAD_DIM, lambda g: heads + g),
            block(rows, HEAD_DIM, lambda g: heads + local_heads + g),
            block(cached, HEAD_DIM, lambda g: g),
            block(cached, HEAD_DIM, lambda g: g),
        ],
        out_specs=block(rows, groups * HEAD_DIM, lambda g: g),
        cost_estimate=pl.CostEstimate(
            flops=4 * heads * rows * (cached + rows) * HEAD_DIM,
            bytes_accessed=4 * heads * rows * HEAD_DIM,
            transcendentals=heads * rows * (cached + rows),
        ),
        compiler_params=pltpu.CompilerParams(vmem_limit_bytes=24 << 20),
        name="attend",
    )(projected, projected, projected, cached_key, cached_value)


def project_kernel(
    chips, cores, picks_ref, owner_ref, rank_ref, gain_ref, kv_ref, h_ref, wq_ref, wk_ref, wv_ref, o_ref, f_ref,
    held, total, hidden, normed, outbox, inbox, forward, copy_sem, ring_send, ring_recv,
    pair_send, pair_recv, peer_send, peer_recv, spread_send, spread_recv, last_send, last_recv,
):
    mesh_id = pl.DeviceIdType.MESH
    me = lax.axis_index("context")
    devices = lax.axis_size("context")
    mine = lax.axis_index("tensor")
    peers = lax.axis_size("tensor")
    core = lax.rem(me, cores)
    chip = me // cores
    length = chips // 2

    def place_to_chip(place):
        side = place // length
        along = (1 - side) * place + side * (chips - 1 - place)
        return 2 * along + side

    side = lax.rem(chip, 2)
    along = chip // 2
    spot = (1 - side) * along + side * (chips - 1 - along)
    right = place_to_chip(lax.rem(spot + 1, chips)) * cores + core
    left = place_to_chip(lax.rem(spot + chips - 1, chips)) * cores + core
    sibling = chip * cores + (cores - 1 - core)

    half = held.shape[4]
    rest = wq_ref.shape[1] - half
    keys = wk_ref.shape[1]
    later = held.at[1, chip, core]
    own = [
        pltpu.make_async_copy(wq_ref.at[:, :half], held.at[0, chip, core], copy_sem.at[0]),
        pltpu.make_async_copy(wq_ref.at[:, half:], later.at[:, :rest], copy_sem.at[1]),
        pltpu.make_async_copy(h_ref, hidden.at[mine], copy_sem.at[2]),
        pltpu.make_async_copy(wk_ref, later.at[:, rest : rest + keys], copy_sem.at[5]),
        pltpu.make_async_copy(wv_ref, later.at[:, rest + keys :], copy_sem.at[6]),
    ]
    for copy in own:
        copy.start()
    barrier = pltpu.get_barrier_semaphore()

    def greet(k, carry):
        pl.semaphore_signal(
            barrier, inc=1, device_id={"context": lax.rem(me + k, devices)}, device_id_type=mesh_id
        )
        return carry

    lax.fori_loop(1, devices, greet, 0)
    for k in range(1, peers):
        pl.semaphore_signal(
            barrier, inc=1, device_id={"tensor": lax.rem(mine + k, peers)}, device_id_type=mesh_id
        )
    pl.semaphore_wait(barrier, devices - 1 + peers - 1)
    for copy in own:
        copy.wait()

    def origin(way, step):
        return place_to_chip(lax.rem(spot + (chips - step if way == 0 else step), chips))

    def ring(way, step, sem):
        piece = held.at[way, origin(way, step), core]
        return pltpu.make_async_remote_copy(
            src_ref=piece,
            dst_ref=piece,
            send_sem=ring_send.at[way, sem],
            recv_sem=ring_recv.at[way, sem],
            device_id={"context": right if way == 0 else left},
            device_id_type=mesh_id,
        )

    def pair(way, step, from_core):
        piece = held.at[way, origin(way, step), from_core]
        return pltpu.make_async_remote_copy(
            src_ref=piece,
            dst_ref=piece,
            send_sem=pair_send.at[way, step],
            recv_sem=pair_recv.at[way, step],
            device_id={"context": sibling},
            device_id_type=mesh_id,
        )

    def peer(k, slot):
        return pltpu.make_async_remote_copy(
            src_ref=hidden.at[slot],
            dst_ref=hidden.at[slot],
            send_sem=peer_send.at[k],
            recv_sem=peer_recv.at[k],
            device_id={"tensor": lax.rem(mine + k, peers)},
            device_id_type=mesh_id,
        )

    def spread(k, slot):
        return pltpu.make_async_remote_copy(
            src_ref=outbox.at[lax.rem(me + k, devices)],
            dst_ref=inbox.at[slot],
            send_sem=spread_send.at[k],
            recv_sem=spread_recv.at[k],
            device_id={"context": lax.rem(me + k, devices)},
            device_id_type=mesh_id,
        )

    def last(k, slot):
        return pltpu.make_async_remote_copy(
            src_ref=forward.at[lax.rem(me + k, devices)],
            dst_ref=f_ref.at[slot],
            send_sem=last_send.at[k],
            recv_sem=last_recv.at[k],
            device_id={"context": lax.rem(me + k, devices)},
            device_id_type=mesh_id,
        )

    def loop(begin, end, action):
        def run(k, carry):
            action(k)
            return carry

        lax.fori_loop(begin, end, run, 0)

    for k in range(1, peers):
        peer(k, mine).start()
    for way in range(2):
        ring(way, 0, 0).start()
        if cores == 2:
            pair(way, 0, core).start()

    def fill(slot):
        outbox[:, slot] = kv_ref[picks_ref[slot]]

    loop(0, MOST_REQ, fill)
    loop(1, devices, lambda k: spread(k, me).start())
    kept = pltpu.make_async_copy(outbox.at[me], inbox.at[me], copy_sem.at[3])
    kept.start()
    total[...] = jnp.zeros_like(total)

    depth = cores * held.shape[3]
    width = 256 if half % 256 == 0 else 128

    def compute(way, step):
        if cores == 2:
            pair(way, step, 1 - core).wait_recv()
        source = origin(way, step)

        def tile(t):
            cols = pl.ds(pl.multiple_of(t * width, width), width)
            block = held[way, source, :, :, cols].reshape(depth, width)
            total[way, :, cols] += jnp.dot(normed[source], block, preferred_element_type=jnp.float32)

        loop(0, half // width, tile)

    def advance(step):
        for way in range(2):
            ring(way, step, step - 1).wait_recv()

            @pl.when(step < chips - 1)
            def _():
                ring(way, step, step).start()

            if cores == 2:
                pair(way, step, core).start()

    loop(1, length - 1, advance)
    for k in range(1, peers):
        peer(k, lax.rem(mine + peers - k, peers)).wait_recv()
    rows = hidden.shape[1]
    part = hidden.shape[2]
    height = min(64, rows)

    def normalise(t):
        at = pl.ds(pl.multiple_of(t * height, height), height)
        squares = jnp.zeros((height, 1), jnp.float32)
        for slot in range(peers):
            floats = hidden[slot, at, :].astype(jnp.float32)
            squares += jnp.sum(floats * floats, axis=1, keepdims=True)
        inverse = lax.rsqrt(squares / (peers * part) + 1e-05)
        for source in range(chips):
            slot, begin = source * depth // part, source * depth % part
            floats = hidden[slot, at, begin : begin + depth].astype(jnp.float32)
            gain = gain_ref[:, source * depth : (source + 1) * depth].astype(jnp.float32)
            normed[source, at, :] = (floats * inverse * gain).astype(jnp.bfloat16)

    loop(0, rows // height, normalise)
    advance(length - 1)
    loop(1, devices, lambda k: spread(k, lax.rem(me + devices - k, devices)).wait_recv())
    kept.wait()

    def relay(listing):
        forward[listing // PICKS, lax.rem(listing, PICKS)] = inbox[
            owner_ref[listing], rank_ref[listing]
        ]

    loop(0, devices * PICKS, relay)
    loop(1, devices, lambda k: last(k, me).start())
    kept_last = pltpu.make_async_copy(forward.at[me], f_ref.at[me], copy_sem.at[4])
    kept_last.start()

    def second(step):
        advance(step)
        for early in range(2):
            for way in range(2):
                compute(way, (step - length) * 2 + early)

    loop(length, chips, second)
    for way in range(2):
        for begin in range(0, half, width):
            o_ref[:, way * half + begin : way * half + begin + width] = total[
                way, :, begin : begin + width
            ].astype(o_ref.dtype)
    loop(1, devices, lambda k: last(k, lax.rem(me + devices - k, devices)).wait_recv())
    kept_last.wait()

    def drain(step):
        for way in range(2):

            @pl.when(step < chips - 1)
            def _():
                ring(way, step, step).wait_send()

            if cores == 2:
                pair(way, step, core).wait_send()

    loop(0, chips, drain)
    loop(1, devices, lambda k: spread(k, me).wait_send())
    loop(1, devices, lambda k: last(k, me).wait_send())
    for k in range(1, peers):
        peer(k, mine).wait_send()


def project(hidden_in, norm_gain, weights, kv_cache, picked, owners, ranks):
    devices = lax.axis_size("context")
    peers = lax.axis_size("tensor")
    cores = 2 if peers == 2 else 1
    chips = devices // cores
    rows, part = hidden_in.shape
    depth = weights[0].shape[0]
    columns = sum(weight.shape[1] for weight in weights)
    half = columns // 2
    span = kv_cache.shape[2]
    piece = C_BLOCK // devices
    smem = pl.BlockSpec(memory_space=pltpu.SMEM)
    vmem = pl.BlockSpec(memory_space=pltpu.VMEM)
    anywhere = pl.BlockSpec(memory_space=pl.ANY)
    sems = lambda *shape: pltpu.SemaphoreType.DMA(shape)
    return pl.pallas_call(
        functools.partial(project_kernel, chips, cores),
        out_shape=(
            jax.ShapeDtypeStruct((rows, columns), jnp.bfloat16),
            jax.ShapeDtypeStruct((devices, PICKS, piece, 2, span), jnp.bfloat16),
        ),
        in_specs=[smem, smem, smem, vmem, vmem, anywhere, anywhere, anywhere, anywhere],
        out_specs=(vmem, vmem),
        scratch_shapes=[
            pltpu.VMEM((2, chips, cores, depth, half), jnp.bfloat16),
            pltpu.VMEM((2, rows, half), jnp.float32),
            pltpu.VMEM((peers, rows, part), jnp.bfloat16),
            pltpu.VMEM((chips, rows, cores * depth), jnp.bfloat16),
            pltpu.VMEM((devices, MOST_REQ, piece, 2, span), jnp.bfloat16),
            pltpu.VMEM((devices, MOST_REQ, piece, 2, span), jnp.bfloat16),
            pltpu.VMEM((devices, PICKS, piece, 2, span), jnp.bfloat16),
            sems(7),
            sems(2, chips),
            sems(2, chips),
            sems(2, chips),
            sems(2, chips),
            sems(peers),
            sems(peers),
            sems(devices),
            sems(devices),
            sems(devices),
            sems(devices),
        ],
        compiler_params=pltpu.CompilerParams(
            collective_id=0, has_side_effects=True, vmem_limit_bytes=58 << 20
        ),
        name="project",
    )(
        picked,
        owners,
        ranks,
        norm_gain.reshape(1, -1),
        kv_cache.reshape(BLOCKS_DEV, devices, piece, 2, span),
        hidden_in,
        *weights,
    )


def on_device(hidden_in, norm_gain, w_query, w_key, w_value, kv_cache, selected):
    local_heads = kv_cache.shape[2] // HEAD_DIM
    groups = w_query.shape[1] // (HEAD_DIM * local_heads)
    devices = lax.axis_size("context")
    weights = (w_query, w_key, w_value)
    owners = (selected // BLOCKS_DEV).reshape(devices * PICKS)
    offsets = (selected % BLOCKS_DEV).reshape(devices * PICKS)
    serial = jnp.arange(devices * PICKS, dtype=jnp.int32)
    earlier = (owners[:, None] == owners[None, :]) & (serial[:, None] > serial[None, :])
    ranks = jnp.sum(earlier.astype(jnp.int32), axis=1)
    slots = jnp.arange(MOST_REQ, dtype=jnp.int32)
    hits = (owners[None, :] == lax.axis_index("context")) & (ranks[None, :] == slots[:, None])
    picked = jnp.sum(jnp.where(hits, offsets[None, :], 0), axis=1)
    projected, fetched = project(hidden_in, norm_gain, weights, kv_cache, picked, owners, ranks)
    fetched = fetched.transpose(1, 0, 2, 3, 4).reshape(PICKS * C_BLOCK, 2, kv_cache.shape[2])
    return attend(projected, fetched[:, 0], fetched[:, 1], groups, local_heads)


LANES = 4
CHUNKS = 4


def plane_kernel(
    planes, groups, plane_ref, spot_ref, picks_ref, gain_ref, kv_ref, h_ref, wq_ref, wk_ref, wv_ref, o_ref,
    wbuf, nb, kvb, kst, pool, flow, ck, cv, prj, ast, gains, sums, copy_sem, wp_send, wp_recv, wz_send, wz_recv,
    sq_send, sq_recv, nx_send, nx_recv, ny_send, ny_recv, nc_send, nc_recv, ca_send, ca_recv, fl_send, fl_recv,
    out_send, out_recv,
):
    mesh_id = pl.DeviceIdType.MESH
    me = lax.axis_index("context")
    y = lax.axis_index("tensor")
    z = me // LANES
    p = lax.rem(me, LANES)
    x, c = p // 2, lax.rem(p, 2)
    last = planes - 1
    rows, part = h_ref.shape
    depth = wq_ref.shape[0]
    hd = HEAD_DIM
    width = groups * hd // 2
    listed = LANES * PICKS
    height = rows // CHUNKS

    def lane(k):
        return lax.rem(x + k // 2, 2) * 2 + lax.rem(c + lax.rem(k, 2), 2)

    def near(k):
        return {"context": z * LANES + lane(k)}

    def loop(begin, end, action):
        def run(k, carry):
            action(k)
            return carry

        lax.fori_loop(begin, end, run, 0)

    def remote(src, dst, send, recv, device):
        return pltpu.make_async_remote_copy(
            src_ref=src, dst_ref=dst, send_sem=send, recv_sem=recv, device_id=device, device_id_type=mesh_id
        )

    across = {"tensor": 1 - y}
    ways = ((z < last, {"context": lax.rem(me + LANES, planes * LANES)}),
            (z > 0, {"context": lax.rem(me + (planes - 1) * LANES, planes * LANES)}))

    def shard(group, pp):
        if group == 0:
            at = pl.ds(pl.multiple_of(pp * hd, hd), hd)
            return ((wk_ref.at[:, at], slice(0, hd)), (wv_ref.at[:, at], slice(hd, 2 * hd)))
        at = pl.ds(pl.multiple_of(pp * 2 * width + (group - 1) * width, hd), width)
        return ((wq_ref.at[:, at], slice(0, width)),)

    own = [
        pltpu.make_async_copy(h_ref, nb.at[y, p], copy_sem.at[0]),
        pltpu.make_async_copy(kv_ref, kvb, copy_sem.at[1]),
    ]
    mine = []
    for group in range(3):
        for at, (src, cols) in enumerate(shard(group, p)):
            mine.append(
                pltpu.make_async_copy(src, wbuf.at[group, z, p, :, cols], copy_sem.at[2 + len(mine)])
            )
    for copy in own + mine:
        copy.start()

    barrier = pltpu.get_barrier_semaphore()
    for k in range(1, LANES):
        pl.semaphore_signal(barrier, inc=1, device_id=near(k), device_id_type=mesh_id)
    pl.semaphore_signal(barrier, inc=1, device_id=across, device_id_type=mesh_id)
    for there, device in ways:

        @pl.when(there)
        def _():
            pl.semaphore_signal(barrier, inc=1, device_id=device, device_id_type=mesh_id)

    pl.semaphore_wait(barrier, LANES + (z < last).astype(jnp.int32) + (z > 0).astype(jnp.int32))

    for group in range(3):
        for k in (2, 3, 1):
            for src, cols in shard(group, lane(k)):
                remote(
                    src, wbuf.at[group, z, p, :, cols], wp_send.at[k, group], wp_recv.at[k, group], near(k)
                ).start()
        for way, (there, device) in enumerate(ways):

            @pl.when(there)
            def _():
                for src, cols in shard(group, p):
                    remote(
                        src, wbuf.at[group, z, p, :, cols], wz_send.at[way, group, z],
                        wz_recv.at[group, z], device,
                    ).start()

    def wp_done(k, group, from_lane):
        piece = wbuf.at[group, z, from_lane]
        return remote(piece, piece, wp_send.at[k, group], wp_recv.at[k, group], near(k))

    def wz(way, group, plane):
        piece = wbuf.at[group, plane]
        return remote(
            piece, piece, wz_send.at[way, group, plane], wz_recv.at[group, plane], ways[way][1]
        )

    def gather_plane(group):
        for k in (1, 2, 3):
            wp_done(k, group, lane(k)).wait_recv()
            piece = wbuf.at[group, z, lane(k)]
            for way, (there, device) in enumerate(ways):

                @pl.when(there)
                def _():
                    remote(
                        piece, piece, wz_send.at[way, group, z], wz_recv.at[group, z], device
                    ).start()

    def forward(group, distance):
        for way in range(2):
            plane = z - distance if way == 0 else z + distance
            inside = plane >= 0 if way == 0 else plane <= last

            @pl.when(inside)
            def _():
                wz(way, group, plane).wait_recv()

                @pl.when(ways[way][0])
                def _():
                    wz(way, group, plane).start()

    own[0].wait()

    def square(t):
        at = pl.ds(pl.multiple_of(t * height, height), height)
        floats = nb[y, p, at, :].astype(jnp.float32)
        total = jnp.sum(floats * floats, axis=1, keepdims=True)
        sums[0, :, at] = jnp.transpose(jnp.broadcast_to(total, (height, 128)))[:8]

    loop(0, CHUNKS, square)
    sq = remote(sums.at[0], sums.at[1], sq_send, sq_recv, across)
    sq.start()

    own[1].wait()

    def pick(slot):
        for kind in range(2):
            block = kvb[picks_ref[slot], :, kind, :]
            for pp in range(LANES):
                kst[pp, slot, kind] = block[:, pp * hd : (pp + 1) * hd]

    loop(0, MOST_REQ, pick)
    slots = pl.ds(p * MOST_REQ, MOST_REQ)

    def cache(k):
        return remote(kst.at[lane(k)], pool.at[slots], ca_send.at[k], ca_recv.at[k], near(k))

    for k in (2, 3, 1):
        cache(k).start()
    kept = pltpu.make_async_copy(kst.at[p], pool.at[slots], copy_sem.at[6])
    kept.start()
    gains[...] = gain_ref[...].astype(jnp.float32)
    sq.wait_recv()

    def nx(t, blk):
        piece = nb.at[y, blk, pl.ds(pl.multiple_of(t * height, height), height)]
        return remote(piece, piece, nx_send.at[t], nx_recv.at[t], near(2))

    def ny(which, t, half, blk):
        piece = nb.at[half, blk, pl.ds(pl.multiple_of(t * height, height), height)]
        return remote(piece, piece, ny_send.at[which, t], ny_recv.at[which, t], across)

    def nc(which, t, half, blk):
        piece = nb.at[half, blk, pl.ds(pl.multiple_of(t * height, height), height)]
        return remote(piece, piece, nc_send.at[which, t], nc_recv.at[which, t], near(1))

    def normalise(t):
        at = pl.ds(pl.multiple_of(t * height, height), height)
        squares = sums[0, 0:1, at] + sums[1, 0:1, at]
        inverse = lax.rsqrt(squares / (2 * part) + 1e-05)
        inverse = jnp.transpose(jnp.broadcast_to(inverse, (128, height)))
        for col in range(part // 128):
            cols = slice(col * 128, (col + 1) * 128)
            gain = gains[pl.ds(y * (part // 128) + col, 1), :]
            floats = nb[y, p, at, cols].astype(jnp.float32)
            nb[y, p, at, cols] = (floats * inverse * gain).astype(jnp.bfloat16)
        nx(t, p).start()
        ny(0, t, y, p).start()
        nc(0, t, y, p).start()

    loop(0, CHUNKS, normalise)
    for copy in mine:
        copy.wait()
    for group in range(3):
        gather_plane(group)

    def bundle(way, plane):
        piece = flow.at[way, plane]
        return remote(piece, piece, fl_send.at[way, plane], fl_recv.at[way, plane], ways[way][1])

    def fill(way, plane):
        def one(d):
            row, col = plane * LANES + d // PICKS, lax.rem(d, PICKS)
            here = plane_ref[row, col] == z
            flow[way, plane, d] = jnp.where(here, pool[spot_ref[row, col]], flow[way, plane, d])

        loop(0, listed, one)

    def stage(step):
        for way in range(2):

            @pl.when(z == (step if way == 0 else last - step))
            def _():
                for hop in range(last - step):
                    plane = last - hop if way == 0 else hop
                    if step > 0:
                        bundle(way, plane).wait_recv()
                    fill(way, plane)
                    bundle(way, plane).start()

    def pass_x(t):
        nx(t, lane(2)).wait_recv()
        ny(1, t, y, lane(2)).start()
        nc(1, t, y, lane(2)).start()

    def pass_y(which, blk):
        def one(t):
            ny(which, t, 1 - y, blk).wait_recv()
            nc(2 + which, t, 1 - y, blk).start()

        loop(0, CHUNKS, one)

    def project(group, k):
        blk = lane(k)
        for begin in range(0, rows, 256):
            at = slice(begin, begin + 256)
            total = jnp.zeros((256, width), jnp.float32)
            for half in range(2):
                weight = wbuf[group, half * planes // 2 : (half + 1) * planes // 2].reshape(part, width)
                total += jnp.dot(nb[half, blk, at, :], weight, preferred_element_type=jnp.float32)
            prj[group, k, at, :] = total.astype(jnp.bfloat16)

    def out(k, half, sender):
        cols = slice(half * width, (half + 1) * width)
        place = pl.ds(pl.multiple_of(sender * 2 * width + half * width, hd), width)
        return remote(
            ast.at[k, :, cols], o_ref.at[:, place], out_send.at[k, half], out_recv.at[k, half], near(k)
        )

    def keep(half):
        cols = slice(half * width, (half + 1) * width)
        place = pl.ds(pl.multiple_of(p * 2 * width + half * width, hd), width)
        return pltpu.make_async_copy(ast.at[0, :, cols], o_ref.at[:, place], copy_sem.at[7 + half])

    def attention(half, k):
        tile = min(ROW_TILE, rows)
        factor = math.log2(math.e) / math.sqrt(hd)
        dims = (((1,), (1,)), ((), ()))
        for head in range(groups // 2):
            place = slice(head * hd, (head + 1) * hd)
            for start in range(0, rows, tile):
                stop = start + tile
                query = prj[1 + half, k, start:stop, place]
                cached = lax.dot_general(query, ck[k], dims, preferred_element_type=jnp.float32)
                fresh = lax.dot_general(
                    query, prj[0, k, :stop, :hd], dims, preferred_element_type=jnp.float32
                )
                row = lax.broadcasted_iota(jnp.int32, fresh.shape, 0) + start
                col = lax.broadcasted_iota(jnp.int32, fresh.shape, 1)
                fresh = jnp.where(col <= row, fresh, -jnp.inf)
                top = jnp.maximum(
                    jnp.max(cached, axis=1, keepdims=True), jnp.max(fresh, axis=1, keepdims=True)
                )
                cached = jnp.exp2((cached - top) * factor)
                fresh = jnp.exp2((fresh - top) * factor)
                total = jnp.sum(cached, axis=1, keepdims=True) + jnp.sum(fresh, axis=1, keepdims=True)
                inverse = 1.0 / total
                mixed = jnp.dot(
                    (cached * inverse).astype(jnp.bfloat16), cv[k], preferred_element_type=jnp.float32
                )
                mixed += jnp.dot(
                    (fresh * inverse).astype(jnp.bfloat16), prj[0, k, :stop, hd:],
                    preferred_element_type=jnp.float32,
                )
                ast[k, start:stop, half * width + head * hd : half * width + (head + 1) * hd] = (
                    mixed.astype(jnp.bfloat16)
                )

        @pl.when(k != 0)
        def _():
            out(k, half, p).start()

        @pl.when(k == 0)
        def _():
            keep(half).start()

    def collect(k):
        for choice in range(PICKS):
            row = z * LANES + lane(k)
            held = plane_ref[row, choice]
            d = lane(k) * PICKS + choice
            block = jnp.where(
                held == z,
                pool[spot_ref[row, choice]],
                jnp.where(held < z, flow[0, z, d], flow[1, z, d]),
            )
            ck[k, choice * C_BLOCK : (choice + 1) * C_BLOCK, :] = block[0]
            cv[k, choice * C_BLOCK : (choice + 1) * C_BLOCK, :] = block[1]

    forward(0, 1)
    forward(1, 1)
    for k in (1, 2, 3):
        remote(kst.at[p], pool.at[pl.ds(lane(k) * MOST_REQ, MOST_REQ)], ca_send.at[k], ca_recv.at[k],
               near(k)).wait_recv()
    kept.wait()
    stage(0)
    for distance in range(2, planes):
        forward(0, distance)
    loop(0, CHUNKS // 2, pass_x)
    pass_y(0, p)
    forward(2, 1)
    for step in range(1, last):
        stage(step)
        if step == 1:
            for distance in range(2, planes):
                forward(1, distance)
    loop(CHUNKS // 2, CHUNKS, pass_x)
    loop(0, CHUNKS, lambda t: nc(0, t, y, lane(1)).wait_recv())
    loop(0, CHUNKS, lambda t: nc(2, t, 1 - y, lane(1)).wait_recv())
    loop(0, 2, lambda k: project(0, k))
    loop(0, 2, lambda k: project(1, k))
    for way in range(2):

        @pl.when(z > 0 if way == 0 else z < last)
        def _():
            bundle(way, z).wait_recv()

    loop(0, LANES, collect)
    loop(0, 2, lambda k: attention(0, k))
    for distance in range(2, planes - 1):
        forward(2, distance)
    pass_y(1, lane(2))
    loop(0, CHUNKS, lambda t: nc(1, t, y, lane(3)).wait_recv())
    loop(0, CHUNKS, lambda t: nc(3, t, 1 - y, lane(3)).wait_recv())
    loop(2, LANES, lambda k: project(0, k))
    loop(2, LANES, lambda k: project(1, k))
    loop(2, LANES, lambda k: attention(0, k))
    forward(2, last)

    def finish(i):
        k = lax.rem(i + 2, LANES)
        project(2, k)
        attention(1, k)

    loop(0, LANES, finish)
    for half in range(2):
        for k in (1, 2, 3):
            out(k, half, lane(k)).wait_recv()
        keep(half).wait()

    for group in range(3):
        for k in range(1, LANES):
            wp_done(k, group, p).wait_send()
        for way in range(2):

            @pl.when(ways[way][0])
            def _():
                def sent(plane):
                    @pl.when(plane <= z if way == 0 else plane >= z)
                    def _():
                        wz(way, group, plane).wait_send()

                loop(0, planes, sent)

    for k in range(1, LANES):
        cache(k).wait_send()
        for half in range(2):
            out(k, half, p).wait_send()
    sq.wait_send()
    for way in range(2):

        def sent(plane):
            @pl.when(plane > z if way == 0 else plane < z)
            def _():
                bundle(way, plane).wait_send()

        loop(0, planes, sent)

    def drain(t):
        nx(t, p).wait_send()
        for which in range(2):
            ny(which, t, y, p).wait_send()
        for which in range(4):
            nc(which, t, y, p).wait_send()

    loop(0, CHUNKS, drain)


def on_plane(hidden_in, norm_gain, w_query, w_key, w_value, kv_cache, selected):
    devices = lax.axis_size("context")
    planes = devices // LANES
    rows, part = hidden_in.shape
    depth = w_query.shape[0]
    groups = w_query.shape[1] // w_key.shape[1]
    width = groups * HEAD_DIM // 2
    owners = lax.shift_right_logical(selected, BLOCKS_DEV.bit_length() - 1)
    offsets = selected & (BLOCKS_DEV - 1)
    serial = lax.broadcasted_iota(jnp.int32, selected.shape, 0) * PICKS + lax.broadcasted_iota(
        jnp.int32, selected.shape, 1
    )
    same = (owners[:, :, None, None] == owners[None, None]) & (serial[:, :, None, None] > serial[None, None])
    ranks = jnp.sum(same.astype(jnp.int32), axis=(2, 3))
    slots = jnp.arange(MOST_REQ, dtype=jnp.int32)
    hits = (owners == lax.axis_index("context"))[None] & (ranks[None] == slots[:, None, None])
    picks = jnp.sum(jnp.where(hits, offsets[None], 0), axis=(1, 2))
    smem = pl.BlockSpec(memory_space=pltpu.SMEM)
    vmem = pl.BlockSpec(memory_space=pltpu.VMEM)
    anywhere = pl.BlockSpec(memory_space=pl.ANY)
    sems = lambda *shape: pltpu.SemaphoreType.DMA(shape)
    both = lambda *shape: [sems(*shape), sems(*shape)]
    bf16 = jnp.bfloat16
    piece = (2, C_BLOCK, HEAD_DIM)
    return pl.pallas_call(
        functools.partial(plane_kernel, planes, groups),
        out_shape=jax.ShapeDtypeStruct((rows, w_query.shape[1]), bf16),
        in_specs=[smem, smem, smem, vmem, anywhere, anywhere, anywhere, anywhere, anywhere],
        out_specs=anywhere,
        scratch_shapes=[
            pltpu.VMEM((3, planes, LANES, depth, width), bf16),
            pltpu.VMEM((2, LANES, rows, part), bf16),
            pltpu.VMEM((BLOCKS_DEV, C_BLOCK, 2, kv_cache.shape[2]), bf16),
            pltpu.VMEM((LANES, MOST_REQ) + piece, bf16),
            pltpu.VMEM((LANES * MOST_REQ,) + piece, bf16),
            pltpu.VMEM((2, planes, LANES * PICKS) + piece, bf16),
            pltpu.VMEM((LANES, PICKS * C_BLOCK, HEAD_DIM), bf16),
            pltpu.VMEM((LANES, PICKS * C_BLOCK, HEAD_DIM), bf16),
            pltpu.VMEM((3, LANES, rows, width), bf16),
            pltpu.VMEM((LANES, rows, 2 * width), bf16),
            pltpu.VMEM((2 * part // 128, 128), jnp.float32),
            pltpu.VMEM((2, 8, rows), jnp.float32),
            sems(9),
            *both(LANES, 3),
            sems(2, 3, planes),
            sems(3, planes),
            pltpu.SemaphoreType.DMA,
            pltpu.SemaphoreType.DMA,
            *both(CHUNKS),
            *both(2, CHUNKS),
            *both(4, CHUNKS),
            *both(LANES),
            *both(2, planes),
            *both(LANES, 2),
        ],
        compiler_params=pltpu.CompilerParams(
            collective_id=1, has_side_effects=True, vmem_limit_bytes=56 << 20
        ),
        name="plane",
    )(
        jnp.right_shift(owners, LANES.bit_length() - 1),
        (owners & (LANES - 1)) * MOST_REQ + ranks,
        picks,
        norm_gain.reshape(-1, 128),
        kv_cache.reshape(BLOCKS_DEV, C_BLOCK, 2, kv_cache.shape[2]),
        hidden_in,
        w_query,
        w_key,
        w_value,
    )


def solution(mesh):
    fits = mesh.shape["tensor"] == 2 and mesh.shape["context"] % (2 * LANES) == 0
    return jax.shard_map(
        on_plane if fits else on_device,
        mesh=mesh,
        in_specs=(
            P("context", "tensor"),
            P(),
            P("context", "tensor"),
            P("context", "tensor"),
            P("context", "tensor"),
            P("context", None, "tensor"),
            P(),
        ),
        out_specs=P("context", "tensor"),
        check_vma=False,
    )
```

```python
import functools
import math

import jax
import jax.numpy as jnp
from jax import lax
from jax.experimental import pallas as pl
from jax.experimental.pallas import tpu as pltpu
from jax.sharding import PartitionSpec as P

HEAD_DIM = 128
C_BLOCK = 128
PICKS = 3
MOST_REQ = 6
BLOCKS_DEV = 8
ROW_TILE = 256


def attend_kernel(groups, q_ref, k_ref, v_ref, ck_ref, cv_ref, o_ref):
    rows = q_ref.shape[0]
    tile = min(ROW_TILE, rows)
    factor = math.log2(math.e) / math.sqrt(HEAD_DIM)
    dims = (((1,), (1,)), ((), ()))
    for head in range(groups):
        place = slice(head * HEAD_DIM, (head + 1) * HEAD_DIM)
        for start in range(0, rows, tile):
            stop = start + tile
            query = q_ref[start:stop, place]
            cached = lax.dot_general(query, ck_ref[...], dims, preferred_element_type=jnp.float32)
            fresh = lax.dot_general(query, k_ref[:stop, :], dims, preferred_element_type=jnp.float32)
            row = lax.broadcasted_iota(jnp.int32, fresh.shape, 0) + start
            col = lax.broadcasted_iota(jnp.int32, fresh.shape, 1)
            fresh = jnp.where(col <= row, fresh, -jnp.inf)
            top = jnp.maximum(
                jnp.max(cached, axis=1, keepdims=True), jnp.max(fresh, axis=1, keepdims=True)
            )
            cached = jnp.exp2((cached - top) * factor)
            fresh = jnp.exp2((fresh - top) * factor)
            total = jnp.sum(cached, axis=1, keepdims=True) + jnp.sum(fresh, axis=1, keepdims=True)
            inverse = 1.0 / total
            mixed = jnp.dot(
                (cached * inverse).astype(jnp.bfloat16),
                cv_ref[...],
                preferred_element_type=jnp.float32,
            )
            mixed += jnp.dot(
                (fresh * inverse).astype(jnp.bfloat16),
                v_ref[:stop, :],
                preferred_element_type=jnp.float32,
            )
            o_ref[start:stop, place] = mixed.astype(o_ref.dtype)


def attend(projected, cached_key, cached_value, groups, local_heads):
    rows = projected.shape[0]
    cached = cached_key.shape[0]
    heads = groups * local_heads
    block = lambda height, width, place: pl.BlockSpec((height, width), lambda g: (0, place(g)))
    return pl.pallas_call(
        functools.partial(attend_kernel, groups),
        grid=(local_heads,),
        out_shape=jax.ShapeDtypeStruct((rows, heads * HEAD_DIM), jnp.bfloat16),
        in_specs=[
            block(rows, groups * HEAD_DIM, lambda g: g),
            block(rows, HEAD_DIM, lambda g: heads + g),
            block(rows, HEAD_DIM, lambda g: heads + local_heads + g),
            block(cached, HEAD_DIM, lambda g: g),
            block(cached, HEAD_DIM, lambda g: g),
        ],
        out_specs=block(rows, groups * HEAD_DIM, lambda g: g),
        cost_estimate=pl.CostEstimate(
            flops=4 * heads * rows * (cached + rows) * HEAD_DIM,
            bytes_accessed=4 * heads * rows * HEAD_DIM,
            transcendentals=heads * rows * (cached + rows),
        ),
        compiler_params=pltpu.CompilerParams(vmem_limit_bytes=24 << 20),
        name="attend",
    )(projected, projected, projected, cached_key, cached_value)


def project_kernel(
    chips, cores, picks_ref, owner_ref, rank_ref, gain_ref, kv_ref, h_ref, wq_ref, wk_ref, wv_ref, o_ref, f_ref,
    held, total, hidden, normed, outbox, inbox, forward, copy_sem, ring_send, ring_recv,
    pair_send, pair_recv, peer_send, peer_recv, spread_send, spread_recv, last_send, last_recv,
):
    mesh_id = pl.DeviceIdType.MESH
    me = lax.axis_index("context")
    devices = lax.axis_size("context")
    mine = lax.axis_index("tensor")
    peers = lax.axis_size("tensor")
    core = lax.rem(me, cores)
    chip = me // cores
    length = chips // 2

    def place_to_chip(place):
        side = place // length
        along = (1 - side) * place + side * (chips - 1 - place)
        return 2 * along + side

    side = lax.rem(chip, 2)
    along = chip // 2
    spot = (1 - side) * along + side * (chips - 1 - along)
    right = place_to_chip(lax.rem(spot + 1, chips)) * cores + core
    left = place_to_chip(lax.rem(spot + chips - 1, chips)) * cores + core
    sibling = chip * cores + (cores - 1 - core)

    half = held.shape[4]
    rest = wq_ref.shape[1] - half
    keys = wk_ref.shape[1]
    later = held.at[1, chip, core]
    own = [
        pltpu.make_async_copy(wq_ref.at[:, :half], held.at[0, chip, core], copy_sem.at[0]),
        pltpu.make_async_copy(wq_ref.at[:, half:], later.at[:, :rest], copy_sem.at[1]),
        pltpu.make_async_copy(h_ref, hidden.at[mine], copy_sem.at[2]),
        pltpu.make_async_copy(wk_ref, later.at[:, rest : rest + keys], copy_sem.at[5]),
        pltpu.make_async_copy(wv_ref, later.at[:, rest + keys :], copy_sem.at[6]),
    ]
    for copy in own:
        copy.start()
    barrier = pltpu.get_barrier_semaphore()

    def greet(k, carry):
        pl.semaphore_signal(
            barrier, inc=1, device_id={"context": lax.rem(me + k, devices)}, device_id_type=mesh_id
        )
        return carry

    lax.fori_loop(1, devices, greet, 0)
    for k in range(1, peers):
        pl.semaphore_signal(
            barrier, inc=1, device_id={"tensor": lax.rem(mine + k, peers)}, device_id_type=mesh_id
        )
    pl.semaphore_wait(barrier, devices - 1 + peers - 1)
    for copy in own:
        copy.wait()

    def origin(way, step):
        return place_to_chip(lax.rem(spot + (chips - step if way == 0 else step), chips))

    def ring(way, step, sem):
        piece = held.at[way, origin(way, step), core]
        return pltpu.make_async_remote_copy(
            src_ref=piece,
            dst_ref=piece,
            send_sem=ring_send.at[way, sem],
            recv_sem=ring_recv.at[way, sem],
            device_id={"context": right if way == 0 else left},
            device_id_type=mesh_id,
        )

    def pair(way, step, from_core):
        piece = held.at[way, origin(way, step), from_core]
        return pltpu.make_async_remote_copy(
            src_ref=piece,
            dst_ref=piece,
            send_sem=pair_send.at[way, step],
            recv_sem=pair_recv.at[way, step],
            device_id={"context": sibling},
            device_id_type=mesh_id,
        )

    def peer(k, slot):
        return pltpu.make_async_remote_copy(
            src_ref=hidden.at[slot],
            dst_ref=hidden.at[slot],
            send_sem=peer_send.at[k],
            recv_sem=peer_recv.at[k],
            device_id={"tensor": lax.rem(mine + k, peers)},
            device_id_type=mesh_id,
        )

    def spread(k, slot):
        return pltpu.make_async_remote_copy(
            src_ref=outbox.at[lax.rem(me + k, devices)],
            dst_ref=inbox.at[slot],
            send_sem=spread_send.at[k],
            recv_sem=spread_recv.at[k],
            device_id={"context": lax.rem(me + k, devices)},
            device_id_type=mesh_id,
        )

    def last(k, slot):
        return pltpu.make_async_remote_copy(
            src_ref=forward.at[lax.rem(me + k, devices)],
            dst_ref=f_ref.at[slot],
            send_sem=last_send.at[k],
            recv_sem=last_recv.at[k],
            device_id={"context": lax.rem(me + k, devices)},
            device_id_type=mesh_id,
        )

    def loop(begin, end, action):
        def run(k, carry):
            action(k)
            return carry

        lax.fori_loop(begin, end, run, 0)

    for k in range(1, peers):
        peer(k, mine).start()
    for way in range(2):
        ring(way, 0, 0).start()
        if cores == 2:
            pair(way, 0, core).start()

    def fill(slot):
        outbox[:, slot] = kv_ref[picks_ref[slot]]

    loop(0, MOST_REQ, fill)
    loop(1, devices, lambda k: spread(k, me).start())
    kept = pltpu.make_async_copy(outbox.at[me], inbox.at[me], copy_sem.at[3])
    kept.start()
    total[...] = jnp.zeros_like(total)

    depth = cores * held.shape[3]
    width = 256 if half % 256 == 0 else 128

    def compute(way, step):
        if cores == 2:
            pair(way, step, 1 - core).wait_recv()
        source = origin(way, step)

        def tile(t):
            cols = pl.ds(pl.multiple_of(t * width, width), width)
            block = held[way, source, :, :, cols].reshape(depth, width)
            total[way, :, cols] += jnp.dot(normed[source], block, preferred_element_type=jnp.float32)

        loop(0, half // width, tile)

    def advance(step):
        for way in range(2):
            ring(way, step, step - 1).wait_recv()

            @pl.when(step < chips - 1)
            def _():
                ring(way, step, step).start()

            if cores == 2:
                pair(way, step, core).start()

    loop(1, length - 1, advance)
    for k in range(1, peers):
        peer(k, lax.rem(mine + peers - k, peers)).wait_recv()
    rows = hidden.shape[1]
    part = hidden.shape[2]
    height = min(64, rows)

    def normalise(t):
        at = pl.ds(pl.multiple_of(t * height, height), height)
        squares = jnp.zeros((height, 1), jnp.float32)
        for slot in range(peers):
            floats = hidden[slot, at, :].astype(jnp.float32)
            squares += jnp.sum(floats * floats, axis=1, keepdims=True)
        inverse = lax.rsqrt(squares / (peers * part) + 1e-05)
        for source in range(chips):
            slot, begin = source * depth // part, source * depth % part
            floats = hidden[slot, at, begin : begin + depth].astype(jnp.float32)
            gain = gain_ref[:, source * depth : (source + 1) * depth].astype(jnp.float32)
            normed[source, at, :] = (floats * inverse * gain).astype(jnp.bfloat16)

    loop(0, rows // height, normalise)
    advance(length - 1)
    loop(1, devices, lambda k: spread(k, lax.rem(me + devices - k, devices)).wait_recv())
    kept.wait()

    def relay(listing):
        forward[listing // PICKS, lax.rem(listing, PICKS)] = inbox[
            owner_ref[listing], rank_ref[listing]
        ]

    loop(0, devices * PICKS, relay)
    loop(1, devices, lambda k: last(k, me).start())
    kept_last = pltpu.make_async_copy(forward.at[me], f_ref.at[me], copy_sem.at[4])
    kept_last.start()

    def second(step):
        advance(step)
        for early in range(2):
            for way in range(2):
                compute(way, (step - length) * 2 + early)

    loop(length, chips, second)
    for way in range(2):
        for begin in range(0, half, width):
            o_ref[:, way * half + begin : way * half + begin + width] = total[
                way, :, begin : begin + width
            ].astype(o_ref.dtype)
    loop(1, devices, lambda k: last(k, lax.rem(me + devices - k, devices)).wait_recv())
    kept_last.wait()

    def drain(step):
        for way in range(2):

            @pl.when(step < chips - 1)
            def _():
                ring(way, step, step).wait_send()

            if cores == 2:
                pair(way, step, core).wait_send()

    loop(0, chips, drain)
    loop(1, devices, lambda k: spread(k, me).wait_send())
    loop(1, devices, lambda k: last(k, me).wait_send())
    for k in range(1, peers):
        peer(k, mine).wait_send()


def project(hidden_in, norm_gain, weights, kv_cache, picked, owners, ranks):
    devices = lax.axis_size("context")
    peers = lax.axis_size("tensor")
    cores = 2 if peers == 2 else 1
    chips = devices // cores
    rows, part = hidden_in.shape
    depth = weights[0].shape[0]
    columns = sum(weight.shape[1] for weight in weights)
    half = columns // 2
    span = kv_cache.shape[2]
    piece = C_BLOCK // devices
    smem = pl.BlockSpec(memory_space=pltpu.SMEM)
    vmem = pl.BlockSpec(memory_space=pltpu.VMEM)
    anywhere = pl.BlockSpec(memory_space=pl.ANY)
    sems = lambda *shape: pltpu.SemaphoreType.DMA(shape)
    return pl.pallas_call(
        functools.partial(project_kernel, chips, cores),
        out_shape=(
            jax.ShapeDtypeStruct((rows, columns), jnp.bfloat16),
            jax.ShapeDtypeStruct((devices, PICKS, piece, 2, span), jnp.bfloat16),
        ),
        in_specs=[smem, smem, smem, vmem, vmem, anywhere, anywhere, anywhere, anywhere],
        out_specs=(vmem, vmem),
        scratch_shapes=[
            pltpu.VMEM((2, chips, cores, depth, half), jnp.bfloat16),
            pltpu.VMEM((2, rows, half), jnp.float32),
            pltpu.VMEM((peers, rows, part), jnp.bfloat16),
            pltpu.VMEM((chips, rows, cores * depth), jnp.bfloat16),
            pltpu.VMEM((devices, MOST_REQ, piece, 2, span), jnp.bfloat16),
            pltpu.VMEM((devices, MOST_REQ, piece, 2, span), jnp.bfloat16),
            pltpu.VMEM((devices, PICKS, piece, 2, span), jnp.bfloat16),
            sems(7),
            sems(2, chips),
            sems(2, chips),
            sems(2, chips),
            sems(2, chips),
            sems(peers),
            sems(peers),
            sems(devices),
            sems(devices),
            sems(devices),
            sems(devices),
        ],
        compiler_params=pltpu.CompilerParams(
            collective_id=0, has_side_effects=True, vmem_limit_bytes=58 << 20
        ),
        name="project",
    )(
        picked,
        owners,
        ranks,
        norm_gain.reshape(1, -1),
        kv_cache.reshape(BLOCKS_DEV, devices, piece, 2, span),
        hidden_in,
        *weights,
    )


def on_device(hidden_in, norm_gain, w_query, w_key, w_value, kv_cache, selected):
    local_heads = kv_cache.shape[2] // HEAD_DIM
    groups = w_query.shape[1] // (HEAD_DIM * local_heads)
    devices = lax.axis_size("context")
    weights = (w_query, w_key, w_value)
    owners = (selected // BLOCKS_DEV).reshape(devices * PICKS)
    offsets = (selected % BLOCKS_DEV).reshape(devices * PICKS)
    serial = jnp.arange(devices * PICKS, dtype=jnp.int32)
    earlier = (owners[:, None] == owners[None, :]) & (serial[:, None] > serial[None, :])
    ranks = jnp.sum(earlier.astype(jnp.int32), axis=1)
    slots = jnp.arange(MOST_REQ, dtype=jnp.int32)
    hits = (owners[None, :] == lax.axis_index("context")) & (ranks[None, :] == slots[:, None])
    picked = jnp.sum(jnp.where(hits, offsets[None, :], 0), axis=1)
    projected, fetched = project(hidden_in, norm_gain, weights, kv_cache, picked, owners, ranks)
    fetched = fetched.transpose(1, 0, 2, 3, 4).reshape(PICKS * C_BLOCK, 2, kv_cache.shape[2])
    return attend(projected, fetched[:, 0], fetched[:, 1], groups, local_heads)


LANES = 4
CHUNKS = 4
PARTS = 2


def plane_kernel(
    planes, groups, plane_ref, spot_ref, picks_ref, gain_ref, kv_ref, h_ref, wq_ref, wk_ref, wv_ref, o_ref,
    w_wide, w_thin, nb, kvb, kst, pool, flow, ck, cv, kv_own, q_wide, q_thin, part_sum, ast, gains, sums, copy_sem, wp_send, wp_recv, wz_send, wz_recv,
    sq_send, sq_recv, nx_send, nx_recv, ny_send, ny_recv, nc_send, nc_recv, ca_send, ca_recv, fl_send, fl_recv,
    out_send, out_recv,
):
    mesh_id = pl.DeviceIdType.MESH
    me = lax.axis_index("context")
    y = lax.axis_index("tensor")
    z = me // LANES
    p = lax.rem(me, LANES)
    x, c = p // 2, lax.rem(p, 2)
    last = planes - 1
    rows, part = h_ref.shape
    depth = wq_ref.shape[0]
    hd = HEAD_DIM
    width = groups * hd // 2
    spans = ((0, width), (width, hd), (width + hd, hd))
    listed = LANES * PICKS
    height = rows // CHUNKS

    def lane(k):
        return lax.rem(x + k // 2, 2) * 2 + lax.rem(c + lax.rem(k, 2), 2)

    def near(k):
        return {"context": z * LANES + lane(k)}

    def loop(begin, end, action):
        def run(k, carry):
            action(k)
            return carry

        lax.fori_loop(begin, end, run, 0)

    def remote(src, dst, send, recv, device):
        return pltpu.make_async_remote_copy(
            src_ref=src, dst_ref=dst, send_sem=send, recv_sem=recv, device_id=device, device_id_type=mesh_id
        )

    across = {"tensor": 1 - y}
    ways = ((z < last, {"context": lax.rem(me + LANES, planes * LANES)}),
            (z > 0, {"context": lax.rem(me + (planes - 1) * LANES, planes * LANES)}))

    def shard(group, pp):
        if group == 0:
            at = pl.ds(pl.multiple_of(pp * hd, hd), hd)
            return ((wk_ref.at[:, at], slice(0, hd)), (wv_ref.at[:, at], slice(hd, 2 * hd)))
        begin, size = spans[group - 1]
        at = pl.ds(pl.multiple_of(pp * 2 * width + begin, hd), size)
        return ((wq_ref.at[:, at], slice(0, size)),)

    def weight(group):
        return w_wide.at[group] if group < 2 else w_thin.at[group - 2]

    own = [
        pltpu.make_async_copy(h_ref, nb.at[y, p], copy_sem.at[0]),
        pltpu.make_async_copy(kv_ref, kvb, copy_sem.at[1]),
    ]
    mine = []
    for group in range(4):
        for src, cols in shard(group, p):
            mine.append(
                pltpu.make_async_copy(src, weight(group).at[z, p, :, cols], copy_sem.at[2 + len(mine)])
            )
    for copy in own + mine:
        copy.start()

    barrier = pltpu.get_barrier_semaphore()
    for k in range(1, LANES):
        pl.semaphore_signal(barrier, inc=1, device_id=near(k), device_id_type=mesh_id)
    pl.semaphore_signal(barrier, inc=1, device_id=across, device_id_type=mesh_id)
    for there, device in ways:

        @pl.when(there)
        def _():
            pl.semaphore_signal(barrier, inc=1, device_id=device, device_id_type=mesh_id)

    pl.semaphore_wait(barrier, LANES + (z < last).astype(jnp.int32) + (z > 0).astype(jnp.int32))

    def send_own(group):
        for way, (there, device) in enumerate(ways):

            @pl.when(there)
            def _():
                for src, cols in shard(group, p):
                    remote(
                        src, weight(group).at[z, p, :, cols], wz_send.at[way, group, z],
                        wz_recv.at[group, z], device,
                    ).start()

    for group in range(4):
        for k in (2, 3, 1):
            for src, cols in shard(group, lane(k)):
                remote(
                    src, weight(group).at[z, p, :, cols], wp_send.at[k, group], wp_recv.at[k, group], near(k)
                ).start()
        if group < 2:
            send_own(group)

    def wp_done(k, group, from_lane):
        piece = weight(group).at[z, from_lane]
        return remote(piece, piece, wp_send.at[k, group], wp_recv.at[k, group], near(k))

    def wz(way, group, plane):
        piece = weight(group).at[plane]
        return remote(
            piece, piece, wz_send.at[way, group, plane], wz_recv.at[group, plane], ways[way][1]
        )

    def gather_plane(group):
        if group >= 2:
            send_own(group)
        for k in (1, 2, 3):
            wp_done(k, group, lane(k)).wait_recv()
            piece = weight(group).at[z, lane(k)]
            for way, (there, device) in enumerate(ways):

                @pl.when(there)
                def _():
                    remote(
                        piece, piece, wz_send.at[way, group, z], wz_recv.at[group, z], device
                    ).start()

    at_end = (z == 0) | (z == last)

    def gather_end(group):
        @pl.when(at_end)
        def _():
            gather_plane(group)

    def gather_inner(group):
        @pl.when(jnp.logical_not(at_end))
        def _():
            gather_plane(group)

    def forward(group, distance):
        for way in range(2):
            plane = z - distance if way == 0 else z + distance
            inside = plane >= 0 if way == 0 else plane <= last

            @pl.when(inside & ways[way][0])
            def _():
                wz(way, group, plane).wait_recv()
                wz(way, group, plane).start()

    def arrive(group, distance):
        for way in range(2):

            @pl.when(z == (last if way == 0 else 0))
            def _():
                wz(way, group, last - distance if way == 0 else distance).wait_recv()

    own[0].wait()

    def square(t):
        at = pl.ds(pl.multiple_of(t * height, height), height)
        floats = nb[y, p, at, :].astype(jnp.float32)
        total = jnp.sum(floats * floats, axis=1, keepdims=True)
        sums[0, :, at] = jnp.transpose(jnp.broadcast_to(total, (height, 128)))[:8]

    loop(0, CHUNKS, square)
    sq = remote(sums.at[0], sums.at[1], sq_send, sq_recv, across)
    sq.start()

    own[1].wait()

    def pick(slot):
        for kind in range(2):
            block = kvb[picks_ref[slot], :, kind, :]
            for pp in range(LANES):
                kst[pp, slot, kind] = block[:, pp * hd : (pp + 1) * hd]

    loop(0, MOST_REQ, pick)
    slots = pl.ds(p * MOST_REQ, MOST_REQ)

    def cache(k):
        return remote(kst.at[lane(k)], pool.at[slots], ca_send.at[k], ca_recv.at[k], near(k))

    for k in (2, 3, 1):
        cache(k).start()
    kept = pltpu.make_async_copy(kst.at[p], pool.at[slots], copy_sem.at[7])
    kept.start()
    gains[...] = gain_ref[...].astype(jnp.float32)
    sq.wait_recv()

    def nx(t, blk):
        piece = nb.at[y, blk, pl.ds(pl.multiple_of(t * height, height), height)]
        return remote(piece, piece, nx_send.at[t], nx_recv.at[t], near(2))

    def ny(which, t, half, blk):
        piece = nb.at[half, blk, pl.ds(pl.multiple_of(t * height, height), height)]
        return remote(piece, piece, ny_send.at[which, t], ny_recv.at[which, t], across)

    def nc(which, t, half, blk):
        piece = nb.at[half, blk, pl.ds(pl.multiple_of(t * height, height), height)]
        return remote(piece, piece, nc_send.at[which, t], nc_recv.at[which, t], near(1))

    def normalise(t):
        at = pl.ds(pl.multiple_of(t * height, height), height)
        squares = sums[0, 0:1, at] + sums[1, 0:1, at]
        inverse = lax.rsqrt(squares / (2 * part) + 1e-05)
        inverse = jnp.transpose(jnp.broadcast_to(inverse, (128, height)))
        for col in range(part // 128):
            cols = slice(col * 128, (col + 1) * 128)
            gain = gains[pl.ds(y * (part // 128) + col, 1), :]
            floats = nb[y, p, at, cols].astype(jnp.float32)
            nb[y, p, at, cols] = (floats * inverse * gain).astype(jnp.bfloat16)
        nx(t, p).start()
        ny(0, t, y, p).start()
        nc(0, t, y, p).start()

    loop(0, CHUNKS, normalise)

    part_size = listed // PARTS

    def bundle(way, plane, h):
        piece = flow.at[way, plane, pl.ds(h * part_size, part_size)]
        return remote(piece, piece, fl_send.at[way, plane, h], fl_recv.at[way, plane, h], ways[way][1])

    def fill(way, plane, h):
        def one(d):
            row, col = plane * LANES + d // PICKS, lax.rem(d, PICKS)
            here = plane_ref[row, col] == z
            flow[way, plane, d] = jnp.where(here, pool[spot_ref[row, col]], flow[way, plane, d])

        loop(h * part_size, (h + 1) * part_size, one)

    def stage(step, hop, h):
        for way in range(2):

            @pl.when(z == (step if way == 0 else last - step))
            def _():
                plane = last - hop if way == 0 else hop
                if step > 0:
                    bundle(way, plane, h).wait_recv()
                fill(way, plane, h)
                bundle(way, plane, h).start()

    def pool_ready():
        for k in (1, 2, 3):
            remote(
                kst.at[p], pool.at[pl.ds(lane(k) * MOST_REQ, MOST_REQ)], ca_send.at[k], ca_recv.at[k], near(k)
            ).wait_recv()
        kept.wait()

    def pass_x(t):
        nx(t, lane(2)).wait_recv()
        if t < CHUNKS - 1:
            ny(1, t, y, lane(2)).start()
        nc(1, t, y, lane(2)).start()

    def over_x(t):
        piece = nb.at[1 - y, p, pl.ds(t * height, height)]
        return remote(piece, piece, ny_send.at[1, t], ny_recv.at[1, t], near(2))

    def pass_y(t):
        ny(0, t, 1 - y, p).wait_recv()
        if t == CHUNKS - 1:
            over_x(t).start()
        nc(2, t, 1 - y, p).start()

    def pass_far(t):
        ny(1, t, 1 - y, lane(2)).wait_recv()
        nc(3, t, 1 - y, lane(2)).start()

    def near_ready():
        for copy in mine:
            copy.wait()
        loop(0, CHUNKS, lambda t: nc(0, t, y, lane(1)).wait_recv())
        loop(0, CHUNKS, lambda t: nc(2, t, 1 - y, lane(1)).wait_recv())

    def far_ready():
        loop(0, CHUNKS, lambda t: nc(1, t, y, lane(3)).wait_recv())
        loop(0, CHUNKS, lambda t: nc(3, t, 1 - y, lane(3)).wait_recv())

    def store(group, k, at, value):
        value = value.astype(jnp.bfloat16)
        if group == 0:
            kv_own[k, at, :] = value
        elif group == 1:
            q_wide[k, at, :] = value
        else:
            q_thin[group - 2, k, at, :] = value

    def project(group, first):
        size = width if group < 2 else hd

        def one(k):
            for begin in range(0, rows, 256):
                at = slice(begin, begin + 256)
                total = jnp.zeros((256, size), jnp.float32)
                for half in range(2):
                    block = weight(group)[half * planes // 2 : (half + 1) * planes // 2].reshape(part, size)
                    total += jnp.dot(nb[half, lane(k), at, :], block, preferred_element_type=jnp.float32)
                store(group, k, at, total)

        loop(first, first + 2, one)

    farthest = jnp.where(z < planes // 2, last, 0)
    share = LANES * depth

    def partial(k, plane, at):
        half = plane // (planes // 2)
        cols = pl.ds(pl.multiple_of(lax.rem(plane, planes // 2) * share, share), share)
        return jnp.dot(
            nb[half, lane(k), at, cols], w_thin[1, plane].reshape(share, hd),
            preferred_element_type=jnp.float32,
        )

    def project_early(first):
        def one(k):
            for begin in range(0, rows, 256):
                at = slice(begin, begin + 256)
                total = jnp.zeros((256, hd), jnp.float32)
                for i in range(last):
                    total += partial(k, i + (z >= planes // 2).astype(jnp.int32), at)
                part_sum[k, at, :] = total

        loop(first, first + 2, one)

    def out(k, group, sender):
        begin, size = spans[group - 1]
        place = pl.ds(pl.multiple_of(sender * 2 * width + begin, hd), size)
        return remote(
            ast.at[k, :, begin : begin + size], o_ref.at[:, place], out_send.at[k, group - 1],
            out_recv.at[k, group - 1], near(k),
        )

    def keep(group):
        begin, size = spans[group - 1]
        place = pl.ds(pl.multiple_of(p * 2 * width + begin, hd), size)
        return pltpu.make_async_copy(
            ast.at[0, :, begin : begin + size], o_ref.at[:, place], copy_sem.at[7 + group]
        )

    def attend_block(group, k):
        tile = min(ROW_TILE, rows)
        factor = math.log2(math.e) / math.sqrt(hd)
        dims = (((1,), (1,)), ((), ()))
        column, size = spans[group - 1]
        for head in range(size // hd):
            place = slice(head * hd, (head + 1) * hd)
            for start in range(0, rows, tile):
                stop = start + tile
                if group == 1:
                    query = q_wide[k, start:stop, place]
                else:
                    query = q_thin[group - 2, k, start:stop, :]
                cached = lax.dot_general(query, ck[k], dims, preferred_element_type=jnp.float32)
                fresh = lax.dot_general(
                    query, kv_own[k, :stop, :hd], dims, preferred_element_type=jnp.float32
                )
                row = lax.broadcasted_iota(jnp.int32, fresh.shape, 0) + start
                col = lax.broadcasted_iota(jnp.int32, fresh.shape, 1)
                fresh = jnp.where(col <= row, fresh, -jnp.inf)
                top = jnp.maximum(
                    jnp.max(cached, axis=1, keepdims=True), jnp.max(fresh, axis=1, keepdims=True)
                )
                cached = jnp.exp2((cached - top) * factor)
                fresh = jnp.exp2((fresh - top) * factor)
                total = jnp.sum(cached, axis=1, keepdims=True) + jnp.sum(fresh, axis=1, keepdims=True)
                inverse = 1.0 / total
                mixed = jnp.dot(
                    (cached * inverse).astype(jnp.bfloat16), cv[k], preferred_element_type=jnp.float32
                )
                mixed += jnp.dot(
                    (fresh * inverse).astype(jnp.bfloat16), kv_own[k, :stop, hd:],
                    preferred_element_type=jnp.float32,
                )
                ast[k, start:stop, column + head * hd : column + (head + 1) * hd] = mixed.astype(jnp.bfloat16)

        @pl.when(k != 0)
        def _():
            out(k, group, p).start()

        @pl.when(k == 0)
        def _():
            keep(group).start()

    def attend_pair(group, first):
        loop(first, first + 2, lambda k: attend_block(group, k))

    def finish(i):
        k = lax.rem(i + 2, LANES)
        for begin in range(0, rows, 256):
            at = slice(begin, begin + 256)
            store(3, k, at, part_sum[k, at, :] + partial(k, farthest, at))
        attend_block(3, k)

    def collect(k):
        for choice in range(PICKS):
            row = z * LANES + lane(k)
            held = plane_ref[row, choice]
            d = lane(k) * PICKS + choice
            block = jnp.where(
                held == z,
                pool[spot_ref[row, choice]],
                jnp.where(held < z, flow[0, z, d], flow[1, z, d]),
            )
            ck[k, choice * C_BLOCK : (choice + 1) * C_BLOCK, :] = block[0]
            cv[k, choice * C_BLOCK : (choice + 1) * C_BLOCK, :] = block[1]

    def collect_all():
        for way in range(2):

            @pl.when(z > 0 if way == 0 else z < last)
            def _():
                for h in range(PARTS):
                    bundle(way, z, h).wait_recv()

        loop(0, LANES, collect)

    def arrive_all(group):
        for distance in range(1, planes):
            arrive(group, distance)

    gather_plane(1)
    gather_plane(0)
    gather_inner(2)
    gather_end(2)
    forward(0, 1)
    pass_y(1)
    pool_ready()
    gather_end(3)
    stage(0, 0, 1)
    forward(2, 1)
    pass_x(0)
    stage(0, 0, 0)
    forward(1, 1)
    forward(0, 2)
    pass_x(1)
    stage(1, 0, 1)
    forward(2, 2)
    stage(0, 1, 1)
    stage(0, 1, 0)
    pass_y(0)
    stage(1, 0, 0)
    pass_far(0)
    forward(1, 2)
    pass_y(2)
    pass_x(2)
    pass_far(1)
    stage(1, 1, 1)
    stage(0, 2, 1)
    pass_y(3)
    near_ready()
    stage(2, 0, 0)
    stage(2, 0, 1)
    gather_inner(3)
    pass_x(3)
    arrive_all(0)
    project(0, 0)
    arrive_all(1)
    project(1, 0)
    stage(0, 2, 0)
    stage(1, 1, 0)
    pass_far(2)
    pass_far(3)
    arrive_all(2)
    project(2, 0)
    far_ready()
    project(1, 2)
    forward(3, 1)
    project(0, 2)
    project(2, 2)
    collect_all()
    attend_pair(1, 2)
    forward(3, 2)
    attend_pair(2, 2)
    attend_pair(1, 0)
    arrive(3, 1)
    arrive(3, 2)
    project_early(0)
    project_early(2)
    arrive(3, 3)
    loop(0, LANES, finish)
    attend_pair(2, 0)
    for group in (1, 2, 3):
        for k in (1, 2, 3):
            out(k, group, lane(k)).wait_recv()
        keep(group).wait()

    for group in range(4):
        for k in range(1, LANES):
            wp_done(k, group, p).wait_send()
        for way in range(2):

            @pl.when(ways[way][0])
            def _():
                def sent(plane):
                    @pl.when(plane <= z if way == 0 else plane >= z)
                    def _():
                        wz(way, group, plane).wait_send()

                loop(0, planes, sent)

    for k in range(1, LANES):
        cache(k).wait_send()
        for group in (1, 2, 3):
            out(k, group, p).wait_send()
    sq.wait_send()
    for way in range(2):

        def sent(plane):
            @pl.when(plane > z if way == 0 else plane < z)
            def _():
                for h in range(PARTS):
                    bundle(way, plane, h).wait_send()

        loop(0, planes, sent)

    def drain(t):
        nx(t, p).wait_send()
        for which in range(2):
            ny(which, t, y, p).wait_send()
        for which in range(4):
            nc(which, t, y, p).wait_send()

    loop(0, CHUNKS, drain)


def on_plane(hidden_in, norm_gain, w_query, w_key, w_value, kv_cache, selected):
    devices = lax.axis_size("context")
    planes = devices // LANES
    rows, part = hidden_in.shape
    depth = w_query.shape[0]
    groups = w_query.shape[1] // w_key.shape[1]
    width = groups * HEAD_DIM // 2
    owners = lax.shift_right_logical(selected, BLOCKS_DEV.bit_length() - 1)
    offsets = selected & (BLOCKS_DEV - 1)
    serial = lax.broadcasted_iota(jnp.int32, selected.shape, 0) * PICKS + lax.broadcasted_iota(
        jnp.int32, selected.shape, 1
    )
    same = (owners[:, :, None, None] == owners[None, None]) & (serial[:, :, None, None] > serial[None, None])
    ranks = jnp.sum(same.astype(jnp.int32), axis=(2, 3))
    slots = jnp.arange(MOST_REQ, dtype=jnp.int32)
    hits = (owners == lax.axis_index("context"))[None] & (ranks[None] == slots[:, None, None])
    picks = jnp.sum(jnp.where(hits, offsets[None], 0), axis=(1, 2))
    smem = pl.BlockSpec(memory_space=pltpu.SMEM)
    vmem = pl.BlockSpec(memory_space=pltpu.VMEM)
    anywhere = pl.BlockSpec(memory_space=pl.ANY)
    sems = lambda *shape: pltpu.SemaphoreType.DMA(shape)
    both = lambda *shape: [sems(*shape), sems(*shape)]
    bf16 = jnp.bfloat16
    piece = (2, C_BLOCK, HEAD_DIM)
    return pl.pallas_call(
        functools.partial(plane_kernel, planes, groups),
        out_shape=jax.ShapeDtypeStruct((rows, w_query.shape[1]), bf16),
        in_specs=[smem, smem, smem, vmem, anywhere, anywhere, anywhere, anywhere, anywhere],
        out_specs=anywhere,
        scratch_shapes=[
            pltpu.VMEM((2, planes, LANES, depth, width), bf16),
            pltpu.VMEM((2, planes, LANES, depth, HEAD_DIM), bf16),
            pltpu.VMEM((2, LANES, rows, part), bf16),
            pltpu.VMEM((BLOCKS_DEV, C_BLOCK, 2, kv_cache.shape[2]), bf16),
            pltpu.VMEM((LANES, MOST_REQ) + piece, bf16),
            pltpu.VMEM((LANES * MOST_REQ,) + piece, bf16),
            pltpu.VMEM((2, planes, LANES * PICKS) + piece, bf16),
            pltpu.VMEM((LANES, PICKS * C_BLOCK, HEAD_DIM), bf16),
            pltpu.VMEM((LANES, PICKS * C_BLOCK, HEAD_DIM), bf16),
            pltpu.VMEM((LANES, rows, 2 * HEAD_DIM), bf16),
            pltpu.VMEM((LANES, rows, width), bf16),
            pltpu.VMEM((2, LANES, rows, HEAD_DIM), bf16),
            pltpu.VMEM((LANES, rows, HEAD_DIM), jnp.float32),
            pltpu.VMEM((LANES, rows, 2 * width), bf16),
            pltpu.VMEM((2 * part // 128, 128), jnp.float32),
            pltpu.VMEM((2, 8, rows), jnp.float32),
            sems(11),
            *both(LANES, 4),
            sems(2, 4, planes),
            sems(4, planes),
            pltpu.SemaphoreType.DMA,
            pltpu.SemaphoreType.DMA,
            *both(CHUNKS),
            *both(2, CHUNKS),
            *both(4, CHUNKS),
            *both(LANES),
            *both(2, planes, PARTS),
            *both(LANES, 3),
        ],
        compiler_params=pltpu.CompilerParams(
            collective_id=1, has_side_effects=True, vmem_limit_bytes=56 << 20
        ),
        name="plane",
    )(
        jnp.right_shift(owners, LANES.bit_length() - 1),
        (owners & (LANES - 1)) * MOST_REQ + ranks,
        picks,
        norm_gain.reshape(-1, 128),
        kv_cache.reshape(BLOCKS_DEV, C_BLOCK, 2, kv_cache.shape[2]),
        hidden_in,
        w_query,
        w_key,
        w_value,
    )


def solution(mesh):
    fits = mesh.shape["tensor"] == 2 and mesh.shape["context"] == 4 * LANES
    return jax.shard_map(
        on_plane if fits else on_device,
        mesh=mesh,
        in_specs=(
            P("context", "tensor"),
            P(),
            P("context", "tensor"),
            P("context", "tensor"),
            P("context", "tensor"),
            P("context", None, "tensor"),
            P(),
        ),
        out_specs=P("context", "tensor"),
        check_vma=False,
    )
```

```python
import functools
import math

import jax
import jax.numpy as jnp
from jax import lax
from jax.experimental import pallas as pl
from jax.experimental.pallas import tpu as pltpu
from jax.sharding import PartitionSpec as P

HEAD_DIM = 128
C_BLOCK = 128
PICKS = 3
MOST_REQ = 6
BLOCKS_DEV = 8
ROW_TILE = 256


def attend_kernel(groups, q_ref, k_ref, v_ref, ck_ref, cv_ref, o_ref):
    rows = q_ref.shape[0]
    tile = min(ROW_TILE, rows)
    factor = math.log2(math.e) / math.sqrt(HEAD_DIM)
    dims = (((1,), (1,)), ((), ()))
    for head in range(groups):
        place = slice(head * HEAD_DIM, (head + 1) * HEAD_DIM)
        for start in range(0, rows, tile):
            stop = start + tile
            query = q_ref[start:stop, place]
            cached = lax.dot_general(query, ck_ref[...], dims, preferred_element_type=jnp.float32)
            fresh = lax.dot_general(query, k_ref[:stop, :], dims, preferred_element_type=jnp.float32)
            row = lax.broadcasted_iota(jnp.int32, fresh.shape, 0) + start
            col = lax.broadcasted_iota(jnp.int32, fresh.shape, 1)
            fresh = jnp.where(col <= row, fresh, -jnp.inf)
            top = jnp.maximum(
                jnp.max(cached, axis=1, keepdims=True), jnp.max(fresh, axis=1, keepdims=True)
            )
            cached = jnp.exp2((cached - top) * factor)
            fresh = jnp.exp2((fresh - top) * factor)
            total = jnp.sum(cached, axis=1, keepdims=True) + jnp.sum(fresh, axis=1, keepdims=True)
            inverse = 1.0 / total
            mixed = jnp.dot(
                (cached * inverse).astype(jnp.bfloat16),
                cv_ref[...],
                preferred_element_type=jnp.float32,
            )
            mixed += jnp.dot(
                (fresh * inverse).astype(jnp.bfloat16),
                v_ref[:stop, :],
                preferred_element_type=jnp.float32,
            )
            o_ref[start:stop, place] = mixed.astype(o_ref.dtype)


def attend(projected, cached_key, cached_value, groups, local_heads):
    rows = projected.shape[0]
    cached = cached_key.shape[0]
    heads = groups * local_heads
    block = lambda height, width, place: pl.BlockSpec((height, width), lambda g: (0, place(g)))
    return pl.pallas_call(
        functools.partial(attend_kernel, groups),
        grid=(local_heads,),
        out_shape=jax.ShapeDtypeStruct((rows, heads * HEAD_DIM), jnp.bfloat16),
        in_specs=[
            block(rows, groups * HEAD_DIM, lambda g: g),
            block(rows, HEAD_DIM, lambda g: heads + g),
            block(rows, HEAD_DIM, lambda g: heads + local_heads + g),
            block(cached, HEAD_DIM, lambda g: g),
            block(cached, HEAD_DIM, lambda g: g),
        ],
        out_specs=block(rows, groups * HEAD_DIM, lambda g: g),
        cost_estimate=pl.CostEstimate(
            flops=4 * heads * rows * (cached + rows) * HEAD_DIM,
            bytes_accessed=4 * heads * rows * HEAD_DIM,
            transcendentals=heads * rows * (cached + rows),
        ),
        compiler_params=pltpu.CompilerParams(vmem_limit_bytes=24 << 20),
        name="attend",
    )(projected, projected, projected, cached_key, cached_value)


def project_kernel(
    chips, cores, picks_ref, owner_ref, rank_ref, gain_ref, kv_ref, h_ref, wq_ref, wk_ref, wv_ref, o_ref, f_ref,
    held, total, hidden, normed, outbox, inbox, forward, copy_sem, ring_send, ring_recv,
    pair_send, pair_recv, peer_send, peer_recv, spread_send, spread_recv, last_send, last_recv,
):
    mesh_id = pl.DeviceIdType.MESH
    me = lax.axis_index("context")
    devices = lax.axis_size("context")
    mine = lax.axis_index("tensor")
    peers = lax.axis_size("tensor")
    core = lax.rem(me, cores)
    chip = me // cores
    length = chips // 2

    def place_to_chip(place):
        side = place // length
        along = (1 - side) * place + side * (chips - 1 - place)
        return 2 * along + side

    side = lax.rem(chip, 2)
    along = chip // 2
    spot = (1 - side) * along + side * (chips - 1 - along)
    right = place_to_chip(lax.rem(spot + 1, chips)) * cores + core
    left = place_to_chip(lax.rem(spot + chips - 1, chips)) * cores + core
    sibling = chip * cores + (cores - 1 - core)

    half = held.shape[4]
    rest = wq_ref.shape[1] - half
    keys = wk_ref.shape[1]
    later = held.at[1, chip, core]
    own = [
        pltpu.make_async_copy(wq_ref.at[:, :half], held.at[0, chip, core], copy_sem.at[0]),
        pltpu.make_async_copy(wq_ref.at[:, half:], later.at[:, :rest], copy_sem.at[1]),
        pltpu.make_async_copy(h_ref, hidden.at[mine], copy_sem.at[2]),
        pltpu.make_async_copy(wk_ref, later.at[:, rest : rest + keys], copy_sem.at[5]),
        pltpu.make_async_copy(wv_ref, later.at[:, rest + keys :], copy_sem.at[6]),
    ]
    for copy in own:
        copy.start()
    barrier = pltpu.get_barrier_semaphore()

    def greet(k, carry):
        pl.semaphore_signal(
            barrier, inc=1, device_id={"context": lax.rem(me + k, devices)}, device_id_type=mesh_id
        )
        return carry

    lax.fori_loop(1, devices, greet, 0)
    for k in range(1, peers):
        pl.semaphore_signal(
            barrier, inc=1, device_id={"tensor": lax.rem(mine + k, peers)}, device_id_type=mesh_id
        )
    pl.semaphore_wait(barrier, devices - 1 + peers - 1)
    for copy in own:
        copy.wait()

    def origin(way, step):
        return place_to_chip(lax.rem(spot + (chips - step if way == 0 else step), chips))

    def ring(way, step, sem):
        piece = held.at[way, origin(way, step), core]
        return pltpu.make_async_remote_copy(
            src_ref=piece,
            dst_ref=piece,
            send_sem=ring_send.at[way, sem],
            recv_sem=ring_recv.at[way, sem],
            device_id={"context": right if way == 0 else left},
            device_id_type=mesh_id,
        )

    def pair(way, step, from_core):
        piece = held.at[way, origin(way, step), from_core]
        return pltpu.make_async_remote_copy(
            src_ref=piece,
            dst_ref=piece,
            send_sem=pair_send.at[way, step],
            recv_sem=pair_recv.at[way, step],
            device_id={"context": sibling},
            device_id_type=mesh_id,
        )

    def peer(k, slot):
        return pltpu.make_async_remote_copy(
            src_ref=hidden.at[slot],
            dst_ref=hidden.at[slot],
            send_sem=peer_send.at[k],
            recv_sem=peer_recv.at[k],
            device_id={"tensor": lax.rem(mine + k, peers)},
            device_id_type=mesh_id,
        )

    def spread(k, slot):
        return pltpu.make_async_remote_copy(
            src_ref=outbox.at[lax.rem(me + k, devices)],
            dst_ref=inbox.at[slot],
            send_sem=spread_send.at[k],
            recv_sem=spread_recv.at[k],
            device_id={"context": lax.rem(me + k, devices)},
            device_id_type=mesh_id,
        )

    def last(k, slot):
        return pltpu.make_async_remote_copy(
            src_ref=forward.at[lax.rem(me + k, devices)],
            dst_ref=f_ref.at[slot],
            send_sem=last_send.at[k],
            recv_sem=last_recv.at[k],
            device_id={"context": lax.rem(me + k, devices)},
            device_id_type=mesh_id,
        )

    def loop(begin, end, action):
        def run(k, carry):
            action(k)
            return carry

        lax.fori_loop(begin, end, run, 0)

    for k in range(1, peers):
        peer(k, mine).start()
    for way in range(2):
        ring(way, 0, 0).start()
        if cores == 2:
            pair(way, 0, core).start()

    def fill(slot):
        outbox[:, slot] = kv_ref[picks_ref[slot]]

    loop(0, MOST_REQ, fill)
    loop(1, devices, lambda k: spread(k, me).start())
    kept = pltpu.make_async_copy(outbox.at[me], inbox.at[me], copy_sem.at[3])
    kept.start()
    total[...] = jnp.zeros_like(total)

    depth = cores * held.shape[3]
    width = 256 if half % 256 == 0 else 128

    def compute(way, step):
        if cores == 2:
            pair(way, step, 1 - core).wait_recv()
        source = origin(way, step)

        def tile(t):
            cols = pl.ds(pl.multiple_of(t * width, width), width)
            block = held[way, source, :, :, cols].reshape(depth, width)
            total[way, :, cols] += jnp.dot(normed[source], block, preferred_element_type=jnp.float32)

        loop(0, half // width, tile)

    def advance(step):
        for way in range(2):
            ring(way, step, step - 1).wait_recv()

            @pl.when(step < chips - 1)
            def _():
                ring(way, step, step).start()

            if cores == 2:
                pair(way, step, core).start()

    loop(1, length - 1, advance)
    for k in range(1, peers):
        peer(k, lax.rem(mine + peers - k, peers)).wait_recv()
    rows = hidden.shape[1]
    part = hidden.shape[2]
    height = min(64, rows)

    def normalise(t):
        at = pl.ds(pl.multiple_of(t * height, height), height)
        squares = jnp.zeros((height, 1), jnp.float32)
        for slot in range(peers):
            floats = hidden[slot, at, :].astype(jnp.float32)
            squares += jnp.sum(floats * floats, axis=1, keepdims=True)
        inverse = lax.rsqrt(squares / (peers * part) + 1e-05)
        for source in range(chips):
            slot, begin = source * depth // part, source * depth % part
            floats = hidden[slot, at, begin : begin + depth].astype(jnp.float32)
            gain = gain_ref[:, source * depth : (source + 1) * depth].astype(jnp.float32)
            normed[source, at, :] = (floats * inverse * gain).astype(jnp.bfloat16)

    loop(0, rows // height, normalise)
    advance(length - 1)
    loop(1, devices, lambda k: spread(k, lax.rem(me + devices - k, devices)).wait_recv())
    kept.wait()

    def relay(listing):
        forward[listing // PICKS, lax.rem(listing, PICKS)] = inbox[
            owner_ref[listing], rank_ref[listing]
        ]

    loop(0, devices * PICKS, relay)
    loop(1, devices, lambda k: last(k, me).start())
    kept_last = pltpu.make_async_copy(forward.at[me], f_ref.at[me], copy_sem.at[4])
    kept_last.start()

    def second(step):
        advance(step)
        for early in range(2):
            for way in range(2):
                compute(way, (step - length) * 2 + early)

    loop(length, chips, second)
    for way in range(2):
        for begin in range(0, half, width):
            o_ref[:, way * half + begin : way * half + begin + width] = total[
                way, :, begin : begin + width
            ].astype(o_ref.dtype)
    loop(1, devices, lambda k: last(k, lax.rem(me + devices - k, devices)).wait_recv())
    kept_last.wait()

    def drain(step):
        for way in range(2):

            @pl.when(step < chips - 1)
            def _():
                ring(way, step, step).wait_send()

            if cores == 2:
                pair(way, step, core).wait_send()

    loop(0, chips, drain)
    loop(1, devices, lambda k: spread(k, me).wait_send())
    loop(1, devices, lambda k: last(k, me).wait_send())
    for k in range(1, peers):
        peer(k, mine).wait_send()


def project(hidden_in, norm_gain, weights, kv_cache, picked, owners, ranks):
    devices = lax.axis_size("context")
    peers = lax.axis_size("tensor")
    cores = 2 if peers == 2 else 1
    chips = devices // cores
    rows, part = hidden_in.shape
    depth = weights[0].shape[0]
    columns = sum(weight.shape[1] for weight in weights)
    half = columns // 2
    span = kv_cache.shape[2]
    piece = C_BLOCK // devices
    smem = pl.BlockSpec(memory_space=pltpu.SMEM)
    vmem = pl.BlockSpec(memory_space=pltpu.VMEM)
    anywhere = pl.BlockSpec(memory_space=pl.ANY)
    sems = lambda *shape: pltpu.SemaphoreType.DMA(shape)
    return pl.pallas_call(
        functools.partial(project_kernel, chips, cores),
        out_shape=(
            jax.ShapeDtypeStruct((rows, columns), jnp.bfloat16),
            jax.ShapeDtypeStruct((devices, PICKS, piece, 2, span), jnp.bfloat16),
        ),
        in_specs=[smem, smem, smem, vmem, vmem, anywhere, anywhere, anywhere, anywhere],
        out_specs=(vmem, vmem),
        scratch_shapes=[
            pltpu.VMEM((2, chips, cores, depth, half), jnp.bfloat16),
            pltpu.VMEM((2, rows, half), jnp.float32),
            pltpu.VMEM((peers, rows, part), jnp.bfloat16),
            pltpu.VMEM((chips, rows, cores * depth), jnp.bfloat16),
            pltpu.VMEM((devices, MOST_REQ, piece, 2, span), jnp.bfloat16),
            pltpu.VMEM((devices, MOST_REQ, piece, 2, span), jnp.bfloat16),
            pltpu.VMEM((devices, PICKS, piece, 2, span), jnp.bfloat16),
            sems(7),
            sems(2, chips),
            sems(2, chips),
            sems(2, chips),
            sems(2, chips),
            sems(peers),
            sems(peers),
            sems(devices),
            sems(devices),
            sems(devices),
            sems(devices),
        ],
        compiler_params=pltpu.CompilerParams(
            collective_id=0, has_side_effects=True, vmem_limit_bytes=58 << 20
        ),
        name="project",
    )(
        picked,
        owners,
        ranks,
        norm_gain.reshape(1, -1),
        kv_cache.reshape(BLOCKS_DEV, devices, piece, 2, span),
        hidden_in,
        *weights,
    )


def on_device(hidden_in, norm_gain, w_query, w_key, w_value, kv_cache, selected):
    local_heads = kv_cache.shape[2] // HEAD_DIM
    groups = w_query.shape[1] // (HEAD_DIM * local_heads)
    devices = lax.axis_size("context")
    weights = (w_query, w_key, w_value)
    owners = (selected // BLOCKS_DEV).reshape(devices * PICKS)
    offsets = (selected % BLOCKS_DEV).reshape(devices * PICKS)
    serial = jnp.arange(devices * PICKS, dtype=jnp.int32)
    earlier = (owners[:, None] == owners[None, :]) & (serial[:, None] > serial[None, :])
    ranks = jnp.sum(earlier.astype(jnp.int32), axis=1)
    slots = jnp.arange(MOST_REQ, dtype=jnp.int32)
    hits = (owners[None, :] == lax.axis_index("context")) & (ranks[None, :] == slots[:, None])
    picked = jnp.sum(jnp.where(hits, offsets[None, :], 0), axis=1)
    projected, fetched = project(hidden_in, norm_gain, weights, kv_cache, picked, owners, ranks)
    fetched = fetched.transpose(1, 0, 2, 3, 4).reshape(PICKS * C_BLOCK, 2, kv_cache.shape[2])
    return attend(projected, fetched[:, 0], fetched[:, 1], groups, local_heads)


LANES = 4
CHUNKS = 4
PARTS = 2


def plane_kernel(
    planes, groups, plane_ref, spot_ref, picks_ref, gain_ref, kv_ref, h_ref, wq_ref, wk_ref, wv_ref, o_ref,
    w_wide, w_thin, nb, kvb, kst, pool, flow, ck, cv, kv_own, q_wide, q_thin, part_sum, ast, gains, sums, copy_sem, wp_send, wp_recv, wz_send, wz_recv,
    sq_send, sq_recv, nx_send, nx_recv, ny_send, ny_recv, nc_send, nc_recv, ca_send, ca_recv, fl_send, fl_recv,
    out_send, out_recv,
):
    mesh_id = pl.DeviceIdType.MESH
    me = lax.axis_index("context")
    y = lax.axis_index("tensor")
    z = me // LANES
    p = lax.rem(me, LANES)
    x, c = p // 2, lax.rem(p, 2)
    last = planes - 1
    rows, part = h_ref.shape
    depth = wq_ref.shape[0]
    hd = HEAD_DIM
    width = groups * hd // 2
    spans = ((0, width), (width, hd), (width + hd, hd))
    listed = LANES * PICKS
    height = rows // CHUNKS

    def lane(k):
        return lax.rem(x + k // 2, 2) * 2 + lax.rem(c + lax.rem(k, 2), 2)

    def near(k):
        return {"context": z * LANES + lane(k)}

    def loop(begin, end, action):
        def run(k, carry):
            action(k)
            return carry

        lax.fori_loop(begin, end, run, 0)

    def remote(src, dst, send, recv, device):
        return pltpu.make_async_remote_copy(
            src_ref=src, dst_ref=dst, send_sem=send, recv_sem=recv, device_id=device, device_id_type=mesh_id
        )

    across = {"tensor": 1 - y}
    ways = ((z < last, {"context": lax.rem(me + LANES, planes * LANES)}),
            (z > 0, {"context": lax.rem(me + (planes - 1) * LANES, planes * LANES)}))

    def shard(group, pp):
        if group == 0:
            at = pl.ds(pl.multiple_of(pp * hd, hd), hd)
            return ((wk_ref.at[:, at], slice(0, hd)), (wv_ref.at[:, at], slice(hd, 2 * hd)))
        begin, size = spans[group - 1]
        at = pl.ds(pl.multiple_of(pp * 2 * width + begin, hd), size)
        return ((wq_ref.at[:, at], slice(0, size)),)

    def weight(group):
        return w_wide.at[group] if group < 2 else w_thin.at[group - 2]

    own = [
        pltpu.make_async_copy(h_ref, nb.at[y, p], copy_sem.at[0]),
        pltpu.make_async_copy(kv_ref, kvb, copy_sem.at[1]),
    ]
    mine = []
    for group in range(4):
        for src, cols in shard(group, p):
            mine.append(
                pltpu.make_async_copy(src, weight(group).at[z, p, :, cols], copy_sem.at[2 + len(mine)])
            )
    for copy in own + mine:
        copy.start()

    barrier = pltpu.get_barrier_semaphore()
    for k in range(1, LANES):
        pl.semaphore_signal(barrier, inc=1, device_id=near(k), device_id_type=mesh_id)
    pl.semaphore_signal(barrier, inc=1, device_id=across, device_id_type=mesh_id)
    for there, device in ways:

        @pl.when(there)
        def _():
            pl.semaphore_signal(barrier, inc=1, device_id=device, device_id_type=mesh_id)

    pl.semaphore_wait(barrier, LANES + (z < last).astype(jnp.int32) + (z > 0).astype(jnp.int32))

    def send_own(group):
        for way, (there, device) in enumerate(ways):

            @pl.when(there)
            def _():
                for src, cols in shard(group, p):
                    remote(
                        src, weight(group).at[z, p, :, cols], wz_send.at[way, group, z],
                        wz_recv.at[group, z], device,
                    ).start()

    for group in range(4):
        for k in (2, 3, 1):
            for src, cols in shard(group, lane(k)):
                remote(
                    src, weight(group).at[z, p, :, cols], wp_send.at[k, group], wp_recv.at[k, group], near(k)
                ).start()
        send_own(group)

    def wp_done(k, group, from_lane):
        piece = weight(group).at[z, from_lane]
        return remote(piece, piece, wp_send.at[k, group], wp_recv.at[k, group], near(k))

    def wz(way, group, plane):
        piece = weight(group).at[plane]
        return remote(
            piece, piece, wz_send.at[way, group, plane], wz_recv.at[group, plane], ways[way][1]
        )

    def gather_plane(group):
        for k in (1, 2, 3):
            wp_done(k, group, lane(k)).wait_recv()
            piece = weight(group).at[z, lane(k)]
            for way, (there, device) in enumerate(ways):

                @pl.when(there)
                def _():
                    remote(
                        piece, piece, wz_send.at[way, group, z], wz_recv.at[group, z], device
                    ).start()

    at_end = (z == 0) | (z == last)

    def gather_end(group):
        @pl.when(at_end)
        def _():
            gather_plane(group)

    def gather_inner(group):
        @pl.when(jnp.logical_not(at_end))
        def _():
            gather_plane(group)

    def forward(group, distance):
        for way in range(2):
            plane = z - distance if way == 0 else z + distance
            inside = plane >= 0 if way == 0 else plane <= last

            @pl.when(inside & ways[way][0])
            def _():
                wz(way, group, plane).wait_recv()
                wz(way, group, plane).start()

    def arrive(group, distance):
        for way in range(2):

            @pl.when(z == (last if way == 0 else 0))
            def _():
                wz(way, group, last - distance if way == 0 else distance).wait_recv()

    def square(t):
        at = pl.ds(pl.multiple_of(t * height, height), height)
        floats = nb[y, p, at, :].astype(jnp.float32)
        total = jnp.sum(floats * floats, axis=1, keepdims=True)
        sums[0, :, at] = jnp.transpose(jnp.broadcast_to(total, (height, 128)))[:8]

    sq = remote(sums.at[0], sums.at[1], sq_send, sq_recv, across)

    def squares():
        own[0].wait()
        loop(0, CHUNKS, square)
        sq.start()

    def pick(slot):
        for kind in range(2):
            block = kvb[picks_ref[slot], :, kind, :]
            for pp in range(LANES):
                kst[pp, slot, kind] = block[:, pp * hd : (pp + 1) * hd]

    slots = pl.ds(p * MOST_REQ, MOST_REQ)

    def cache(k):
        return remote(kst.at[lane(k)], pool.at[slots], ca_send.at[k], ca_recv.at[k], near(k))

    kept = pltpu.make_async_copy(kst.at[p], pool.at[slots], copy_sem.at[7])

    def pick_all():
        own[1].wait()
        loop(0, MOST_REQ, pick)
        for k in (2, 3, 1):
            cache(k).start()
        kept.start()

    def nx(t, blk):
        piece = nb.at[y, blk, pl.ds(pl.multiple_of(t * height, height), height)]
        return remote(piece, piece, nx_send.at[t], nx_recv.at[t], near(2))

    def ny(which, t, half, blk):
        piece = nb.at[half, blk, pl.ds(pl.multiple_of(t * height, height), height)]
        return remote(piece, piece, ny_send.at[which, t], ny_recv.at[which, t], across)

    def nc(which, t, half, blk):
        piece = nb.at[half, blk, pl.ds(pl.multiple_of(t * height, height), height)]
        return remote(piece, piece, nc_send.at[which, t], nc_recv.at[which, t], near(1))

    def normalise(t):
        if t == 0:
            gains[...] = gain_ref[...].astype(jnp.float32)
            sq.wait_recv()
        at = pl.ds(pl.multiple_of(t * height, height), height)
        squares = sums[0, 0:1, at] + sums[1, 0:1, at]
        inverse = lax.rsqrt(squares / (2 * part) + 1e-05)
        inverse = jnp.transpose(jnp.broadcast_to(inverse, (128, height)))
        for col in range(part // 128):
            cols = slice(col * 128, (col + 1) * 128)
            gain = gains[pl.ds(y * (part // 128) + col, 1), :]
            floats = nb[y, p, at, cols].astype(jnp.float32)
            nb[y, p, at, cols] = (floats * inverse * gain).astype(jnp.bfloat16)
        nx(t, p).start()
        ny(0, t, y, p).start()
        nc(0, t, y, p).start()


    part_size = listed // PARTS

    def bundle(way, plane, h):
        piece = flow.at[way, plane, pl.ds(h * part_size, part_size)]
        return remote(piece, piece, fl_send.at[way, plane, h], fl_recv.at[way, plane, h], ways[way][1])

    def fill(way, plane, h):
        def one(d):
            row, col = plane * LANES + d // PICKS, lax.rem(d, PICKS)
            here = plane_ref[row, col] == z
            flow[way, plane, d] = jnp.where(here, pool[spot_ref[row, col]], flow[way, plane, d])

        loop(h * part_size, (h + 1) * part_size, one)

    def stage(step, hop, h):
        for way in range(2):

            @pl.when(z == (step if way == 0 else last - step))
            def _():
                plane = last - hop if way == 0 else hop
                if step > 0:
                    bundle(way, plane, h).wait_recv()
                fill(way, plane, h)
                bundle(way, plane, h).start()

    def pool_ready():
        for k in (1, 2, 3):
            remote(
                kst.at[p], pool.at[pl.ds(lane(k) * MOST_REQ, MOST_REQ)], ca_send.at[k], ca_recv.at[k], near(k)
            ).wait_recv()
        kept.wait()

    def pass_x(t):
        nx(t, lane(2)).wait_recv()
        if t < CHUNKS - 1:
            ny(1, t, y, lane(2)).start()
        nc(1, t, y, lane(2)).start()

    def over_x(t):
        piece = nb.at[1 - y, p, pl.ds(t * height, height)]
        return remote(piece, piece, ny_send.at[1, t], ny_recv.at[1, t], near(2))

    def pass_y(t):
        ny(0, t, 1 - y, p).wait_recv()
        if t == CHUNKS - 1:
            over_x(t).start()
        nc(2, t, 1 - y, p).start()

    def pass_far(t):
        ny(1, t, 1 - y, lane(2)).wait_recv()
        nc(3, t, 1 - y, lane(2)).start()

    def near_ready():
        for copy in mine:
            copy.wait()
        loop(0, CHUNKS, lambda t: nc(0, t, y, lane(1)).wait_recv())
        loop(0, CHUNKS, lambda t: nc(2, t, 1 - y, lane(1)).wait_recv())

    def far_ready():
        loop(0, CHUNKS, lambda t: nc(1, t, y, lane(3)).wait_recv())
        loop(0, CHUNKS, lambda t: nc(3, t, 1 - y, lane(3)).wait_recv())

    def store(group, k, at, value):
        value = value.astype(jnp.bfloat16)
        if group == 0:
            kv_own[k, at, :] = value
        elif group == 1:
            q_wide[k, at, :] = value
        else:
            q_thin[group - 2, k, at, :] = value

    def project(group, first):
        size = width if group < 2 else hd

        def one(k):
            for begin in range(0, rows, 256):
                at = slice(begin, begin + 256)
                total = jnp.zeros((256, size), jnp.float32)
                for half in range(2):
                    block = weight(group)[half * planes // 2 : (half + 1) * planes // 2].reshape(part, size)
                    total += jnp.dot(nb[half, lane(k), at, :], block, preferred_element_type=jnp.float32)
                store(group, k, at, total)

        loop(first, first + 2, one)

    farthest = jnp.where(z < planes // 2, last, 0)
    share = LANES * depth

    def partial(k, plane, at):
        half = plane // (planes // 2)
        cols = pl.ds(pl.multiple_of(lax.rem(plane, planes // 2) * share, share), share)
        return jnp.dot(
            nb[half, lane(k), at, cols], w_thin[1, plane].reshape(share, hd),
            preferred_element_type=jnp.float32,
        )

    def project_early(first):
        def one(k):
            for begin in range(0, rows, 256):
                at = slice(begin, begin + 256)
                total = jnp.zeros((256, hd), jnp.float32)
                for i in range(last):
                    total += partial(k, i + (z >= planes // 2).astype(jnp.int32), at)
                part_sum[k, at, :] = total

        loop(first, first + 2, one)

    def out(k, group, sender):
        begin, size = spans[group - 1]
        place = pl.ds(pl.multiple_of(sender * 2 * width + begin, hd), size)
        return remote(
            ast.at[k, :, begin : begin + size], o_ref.at[:, place], out_send.at[k, group - 1],
            out_recv.at[k, group - 1], near(k),
        )

    def keep(group):
        begin, size = spans[group - 1]
        place = pl.ds(pl.multiple_of(p * 2 * width + begin, hd), size)
        return pltpu.make_async_copy(
            ast.at[0, :, begin : begin + size], o_ref.at[:, place], copy_sem.at[7 + group]
        )

    def attend_block(group, k):
        tile = min(ROW_TILE, rows)
        factor = math.log2(math.e) / math.sqrt(hd)
        dims = (((1,), (1,)), ((), ()))
        column, size = spans[group - 1]
        for head in range(size // hd):
            place = slice(head * hd, (head + 1) * hd)
            for start in range(0, rows, tile):
                stop = start + tile
                if group == 1:
                    query = q_wide[k, start:stop, place]
                else:
                    query = q_thin[group - 2, k, start:stop, :]
                cached = lax.dot_general(query, ck[k], dims, preferred_element_type=jnp.float32)
                fresh = lax.dot_general(
                    query, kv_own[k, :stop, :hd], dims, preferred_element_type=jnp.float32
                )
                row = lax.broadcasted_iota(jnp.int32, fresh.shape, 0) + start
                col = lax.broadcasted_iota(jnp.int32, fresh.shape, 1)
                fresh = jnp.where(col <= row, fresh, -jnp.inf)
                top = jnp.maximum(
                    jnp.max(cached, axis=1, keepdims=True), jnp.max(fresh, axis=1, keepdims=True)
                )
                cached = jnp.exp2((cached - top) * factor)
                fresh = jnp.exp2((fresh - top) * factor)
                total = jnp.sum(cached, axis=1, keepdims=True) + jnp.sum(fresh, axis=1, keepdims=True)
                inverse = 1.0 / total
                mixed = jnp.dot(
                    (cached * inverse).astype(jnp.bfloat16), cv[k], preferred_element_type=jnp.float32
                )
                mixed += jnp.dot(
                    (fresh * inverse).astype(jnp.bfloat16), kv_own[k, :stop, hd:],
                    preferred_element_type=jnp.float32,
                )
                ast[k, start:stop, column + head * hd : column + (head + 1) * hd] = mixed.astype(jnp.bfloat16)

        @pl.when(k != 0)
        def _():
            out(k, group, p).start()

        @pl.when(k == 0)
        def _():
            keep(group).start()

    def attend_pair(group, first):
        loop(first, first + 2, lambda k: attend_block(group, k))

    def finish(i):
        k = lax.rem(i + 2, LANES)
        for begin in range(0, rows, 256):
            at = slice(begin, begin + 256)
            store(3, k, at, part_sum[k, at, :] + partial(k, farthest, at))
        attend_block(3, k)

    def collect(k):
        for choice in range(PICKS):
            row = z * LANES + lane(k)
            held = plane_ref[row, choice]
            d = lane(k) * PICKS + choice
            block = jnp.where(
                held == z,
                pool[spot_ref[row, choice]],
                jnp.where(held < z, flow[0, z, d], flow[1, z, d]),
            )
            ck[k, choice * C_BLOCK : (choice + 1) * C_BLOCK, :] = block[0]
            cv[k, choice * C_BLOCK : (choice + 1) * C_BLOCK, :] = block[1]

    def collect_all():
        for way in range(2):

            @pl.when(z > 0 if way == 0 else z < last)
            def _():
                for h in range(PARTS):
                    bundle(way, z, h).wait_recv()

        loop(0, LANES, collect)

    def arrive_all(group):
        for distance in range(1, planes):
            arrive(group, distance)

    squares()
    normalise(0)
    gather_plane(0)
    pick_all()
    gather_end(2)
    gather_plane(1)
    normalise(1)
    forward(0, 1)
    pass_y(0)
    normalise(2)
    gather_inner(2)
    gather_end(3)
    forward(1, 1)
    normalise(3)
    forward(2, 1)
    pass_x(0)
    pass_y(1)
    pool_ready()
    stage(0, 0, 0)
    forward(0, 2)
    pass_y(2)
    stage(0, 0, 1)
    forward(2, 2)
    pass_y(3)
    stage(0, 1, 0)
    stage(1, 0, 0)
    forward(1, 2)
    pass_x(1)
    stage(0, 1, 1)
    stage(0, 2, 0)
    near_ready()
    pass_x(2)
    stage(1, 0, 1)
    stage(0, 2, 1)
    stage(2, 0, 0)
    arrive_all(2)
    project(2, 0)
    stage(1, 1, 0)
    arrive_all(0)
    project(0, 0)
    pass_x(3)
    pass_far(1)
    pass_far(0)
    stage(2, 0, 1)
    gather_inner(3)
    arrive_all(1)
    project(1, 0)
    pass_far(2)
    stage(1, 1, 1)
    pass_far(3)
    far_ready()
    project(1, 2)
    project(0, 2)
    collect_all()
    forward(3, 1)
    attend_pair(1, 2)
    attend_pair(2, 0)
    project(2, 2)
    forward(3, 2)
    attend_pair(2, 2)
    arrive(3, 1)
    arrive(3, 2)
    project_early(0)
    project_early(2)
    arrive(3, 3)
    loop(0, 2, finish)
    attend_pair(1, 0)
    loop(2, LANES, finish)
    for group in (1, 2, 3):
        for k in (1, 2, 3):
            out(k, group, lane(k)).wait_recv()
        keep(group).wait()

    for group in range(4):
        for k in range(1, LANES):
            wp_done(k, group, p).wait_send()
        for way in range(2):

            @pl.when(ways[way][0])
            def _():
                def sent(plane):
                    @pl.when(plane <= z if way == 0 else plane >= z)
                    def _():
                        wz(way, group, plane).wait_send()

                loop(0, planes, sent)

    for k in range(1, LANES):
        cache(k).wait_send()
        for group in (1, 2, 3):
            out(k, group, p).wait_send()
    sq.wait_send()
    for way in range(2):

        def sent(plane):
            @pl.when(plane > z if way == 0 else plane < z)
            def _():
                for h in range(PARTS):
                    bundle(way, plane, h).wait_send()

        loop(0, planes, sent)

    def drain(t):
        nx(t, p).wait_send()
        for which in range(2):
            ny(which, t, y, p).wait_send()
        for which in range(4):
            nc(which, t, y, p).wait_send()

    loop(0, CHUNKS, drain)


def on_plane(hidden_in, norm_gain, w_query, w_key, w_value, kv_cache, selected):
    devices = lax.axis_size("context")
    planes = devices // LANES
    rows, part = hidden_in.shape
    depth = w_query.shape[0]
    groups = w_query.shape[1] // w_key.shape[1]
    width = groups * HEAD_DIM // 2
    owners = lax.shift_right_logical(selected, BLOCKS_DEV.bit_length() - 1)
    offsets = selected & (BLOCKS_DEV - 1)
    serial = lax.broadcasted_iota(jnp.int32, selected.shape, 0) * PICKS + lax.broadcasted_iota(
        jnp.int32, selected.shape, 1
    )
    same = (owners[:, :, None, None] == owners[None, None]) & (serial[:, :, None, None] > serial[None, None])
    ranks = jnp.sum(same.astype(jnp.int32), axis=(2, 3))
    slots = jnp.arange(MOST_REQ, dtype=jnp.int32)
    hits = (owners == lax.axis_index("context"))[None] & (ranks[None] == slots[:, None, None])
    picks = jnp.sum(jnp.where(hits, offsets[None], 0), axis=(1, 2))
    smem = pl.BlockSpec(memory_space=pltpu.SMEM)
    vmem = pl.BlockSpec(memory_space=pltpu.VMEM)
    anywhere = pl.BlockSpec(memory_space=pl.ANY)
    sems = lambda *shape: pltpu.SemaphoreType.DMA(shape)
    both = lambda *shape: [sems(*shape), sems(*shape)]
    bf16 = jnp.bfloat16
    piece = (2, C_BLOCK, HEAD_DIM)
    return pl.pallas_call(
        functools.partial(plane_kernel, planes, groups),
        out_shape=jax.ShapeDtypeStruct((rows, w_query.shape[1]), bf16),
        in_specs=[smem, smem, smem, vmem, anywhere, anywhere, anywhere, anywhere, anywhere],
        out_specs=anywhere,
        scratch_shapes=[
            pltpu.VMEM((2, planes, LANES, depth, width), bf16),
            pltpu.VMEM((2, planes, LANES, depth, HEAD_DIM), bf16),
            pltpu.VMEM((2, LANES, rows, part), bf16),
            pltpu.VMEM((BLOCKS_DEV, C_BLOCK, 2, kv_cache.shape[2]), bf16),
            pltpu.VMEM((LANES, MOST_REQ) + piece, bf16),
            pltpu.VMEM((LANES * MOST_REQ,) + piece, bf16),
            pltpu.VMEM((2, planes, LANES * PICKS) + piece, bf16),
            pltpu.VMEM((LANES, PICKS * C_BLOCK, HEAD_DIM), bf16),
            pltpu.VMEM((LANES, PICKS * C_BLOCK, HEAD_DIM), bf16),
            pltpu.VMEM((LANES, rows, 2 * HEAD_DIM), bf16),
            pltpu.VMEM((LANES, rows, width), bf16),
            pltpu.VMEM((2, LANES, rows, HEAD_DIM), bf16),
            pltpu.VMEM((LANES, rows, HEAD_DIM), jnp.float32),
            pltpu.VMEM((LANES, rows, 2 * width), bf16),
            pltpu.VMEM((2 * part // 128, 128), jnp.float32),
            pltpu.VMEM((2, 8, rows), jnp.float32),
            sems(11),
            *both(LANES, 4),
            sems(2, 4, planes),
            sems(4, planes),
            pltpu.SemaphoreType.DMA,
            pltpu.SemaphoreType.DMA,
            *both(CHUNKS),
            *both(2, CHUNKS),
            *both(4, CHUNKS),
            *both(LANES),
            *both(2, planes, PARTS),
            *both(LANES, 3),
        ],
        compiler_params=pltpu.CompilerParams(
            collective_id=1, has_side_effects=True, vmem_limit_bytes=56 << 20
        ),
        name="plane",
    )(
        jnp.right_shift(owners, LANES.bit_length() - 1),
        (owners & (LANES - 1)) * MOST_REQ + ranks,
        picks,
        norm_gain.reshape(-1, 128),
        kv_cache.reshape(BLOCKS_DEV, C_BLOCK, 2, kv_cache.shape[2]),
        hidden_in,
        w_query,
        w_key,
        w_value,
    )


def solution(mesh):
    fits = mesh.shape["tensor"] == 2 and mesh.shape["context"] == 4 * LANES
    return jax.shard_map(
        on_plane if fits else on_device,
        mesh=mesh,
        in_specs=(
            P("context", "tensor"),
            P(),
            P("context", "tensor"),
            P("context", "tensor"),
            P("context", "tensor"),
            P("context", None, "tensor"),
            P(),
        ),
        out_specs=P("context", "tensor"),
        check_vma=False,
    )
```
